32 devices in a mesh: dp: 4 (over z), tensor: 8 (over y, x, core).
Axes of the slice: x: 2, y: 2, z: 4, core: 2. Of those that a mesh axis runs over, the one named last changes fastest.
Arguments:
- frames: bfloat16 [4, 16, 1024, 512], P(None, 'dp'), may hold values from -6 to 6
- cotangent: bfloat16 [4, 16, 1024, 512], P(None, 'dp'), may hold values from -6 to 6
- lengths: int32 [4, 16], P(None, 'dp'), may hold values from 1 to 1024, 12288 in all within a row
- expand_weight: float32 [512, 1536], P('dp', 'tensor'), may hold values from -0.25 to 0.25
- expand_first: float32 [512, 1536], P('dp', 'tensor'), may hold values from -384 to 384
- expand_second: float32 [512, 1536], P('dp', 'tensor'), may hold values from 3932.16 to 29491.2
- project_weight: float32 [1536, 512], P('tensor', 'dp'), may hold values from -0.15625 to 0.15625
- project_first: float32 [1536, 512], P('tensor', 'dp'), may hold values from -640 to 640
- project_second: float32 [1536, 512], P('tensor', 'dp'), may hold values from 9830.4 to 58982.4
- hidden_bias: float32 [1536], P('tensor'), may hold values from -3 to 3
- hidden_bias_first: float32 [1536], P('tensor'), may hold values from -384 to 384
- hidden_bias_second: float32 [1536], P('tensor'), may hold values from 3932.16 to 29491.2
- channel_param: float32 [12, 512], P(None, 'dp'), may hold values from -2 to 2
- channel_first: float32 [12, 512], P(None, 'dp'), may hold values from -768 to 768
- channel_second: float32 [12, 512], P(None, 'dp'), may hold values from 9830.4 to 73728
Outputs:
- block_out: bfloat16 [4, 16, 1024, 512], P(None, 'dp')
- frames_grad: bfloat16 [4, 16, 1024, 512], P(None, 'dp')
- expand_new: float32 [512, 1536], P('dp', 'tensor')
- expand_first_new: float32 [512, 1536], P('dp', 'tensor')
- expand_second_new: float32 [512, 1536], P('dp', 'tensor')
- expand_low: bfloat16 [512, 1536], P('dp', 'tensor')
- project_new: float32 [1536, 512], P('tensor', 'dp')
- project_first_new: float32 [1536, 512], P('tensor', 'dp')
- project_second_new: float32 [1536, 512], P('tensor', 'dp')
- project_low: bfloat16 [1536, 512], P('tensor', 'dp')
- bias_new: float32 [1536], P('tensor')
- bias_first_new: float32 [1536], P('tensor')
- bias_second_new: float32 [1536], P('tensor')
- channel_new: float32 [12, 512], P(None, 'dp')
- channel_first_new: float32 [12, 512], P(None, 'dp')
- channel_second_new: float32 [12, 512], P(None, 'dp')
The draws below stay inside these ranges and needn't reach their ends.
Inputs may be any that keep to these rules, and one draw needn't show every extreme that they name: `lengths`: in each micro-batch the 16 true frame counts sum to 12288 and the largest is 1024.
All inputs are finite; a program needn't handle non-finite values. No bound on the sum of `lengths` on one device may be relied on, other than what follows from the above.
Results may differ from the reference program's by a relative error of at most 0.015.
Values may be sent and summed in bfloat16 or wider, within the bound.
A program may use at most 512 MiB of HBM per device.

```python
import math
import jax
import jax.numpy as jnp
import numpy as np
from jax import lax

C = 512
H = 1536
MB = 4
L = 1024
CL = 4
CLIPS = 16
FRAMES = 49152


def draw_channel_param(key, part):
    keys = jax.random.split(jax.random.fold_in(key, 11), 6)
    taps = 0.4 * jax.random.normal(keys[0], (7, C), jnp.float32)
    kernel_bias = 0.3 * jax.random.normal(keys[1], (1, C), jnp.float32)
    norm_gain = jax.random.uniform(keys[2], (1, C), jnp.float32, 0.6, 1.4)
    norm_shift = 0.3 * jax.random.normal(keys[3], (1, C), jnp.float32)
    out_bias = 0.3 * jax.random.normal(keys[4], (1, C), jnp.float32)
    layer_scale = jax.random.uniform(keys[5], (1, C), jnp.float32, 0.6, 1.4)
    stacked = jnp.concatenate([taps, kernel_bias, norm_gain, norm_shift, out_bias, layer_scale], axis=0)
    return jnp.clip(stacked, -2.0, 2.0)


def level_of(own_key, shape, pieces, least, largest):
    factor_of, own = 1.0, jax.random.fold_in(own_key, 6)
    for dim, parts in pieces:
        steps = jnp.exp(jax.random.uniform(jax.random.fold_in(own, dim), (parts,), jnp.float32, least / len(pieces), largest / len(pieces)))
        factor_of = factor_of * jnp.repeat(steps, shape[dim] // parts).reshape([-1 if axis == dim else 1 for axis in range(len(shape))])
    return factor_of


def split_up(count, total, most, lean):
    weights = [(1 << 20) // math.isqrt(rank ** lean) + 1 for rank in range(2, count + 1)]
    spare, holding = total - most - (count - 1), [1] * (count - 1)
    while spare > 0:
        free = [i for i in range(count - 1) if holding[i] < most]
        mass, remaining = sum([weights[i] for i in free]), spare
        for i in free:
            addition = min(most - holding[i], max(1, remaining * weights[i] // mass), spare)
            holding[i] = holding[i] + addition
            spare = spare - addition
    return np.array([most] + holding)


def ragged(own_key, amount, total, reach, lean):
    if amount == 2:
        one = jax.random.randint(own_key, (), max(1, total - reach), min(reach, total - 1) + 1)
        return jnp.stack([one, total - one])
    sizes = jnp.asarray(split_up(amount, total, reach, lean), jnp.int32)
    pairs = (amount - 1) // 2
    giver, receiver = sizes[1:1 + 2 * pairs:2], sizes[2:2 + 2 * pairs:2]
    margin = jnp.minimum(giver - 1, reach - receiver)
    shifted = jax.random.randint(jax.random.fold_in(own_key, 1), (pairs,), 0, 1 << 20) % (margin + 1)
    sizes = sizes.at[1:1 + 2 * pairs:2].set(giver - shifted).at[2:2 + 2 * pairs:2].set(receiver + shifted)
    return sizes[jax.random.permutation(jax.random.fold_in(own_key, 2), amount)]


def scatter_about(rng, extent, scale, limit, shards=(), held_as=jnp.bfloat16):
    drawn = jax.random.normal(rng, extent, jnp.float32) * scale
    if len(shards) > 0:
        drawn = level_of(rng, extent, shards, -0.22, 0.18) * drawn
    return jnp.clip(drawn, min=-limit, max=limit).astype(held_as)


def setup_inputs(seed: int = 0) -> dict:
    key_list = jax.random.split(jax.random.key(seed), 16)
    frames = scatter_about(key_list[0], (MB, CLIPS, L, C), 1.0, 6.0, ((1, 4),))
    cotangent = scatter_about(key_list[1], (MB, CLIPS, L, C), 1.0, 6.0, ((1, 4),))
    lengths = jax.vmap(lambda own: ragged(own, CLIPS, 3 * CLIPS * L // 4, L, 2))(jax.random.split(key_list[2], MB)).reshape((MB, CLIPS)).astype(jnp.int32)
    expand_weight = scatter_about(key_list[3], (C, H), C ** -0.5, 0.25, ((0, 4), (1, 8)), jnp.float32)
    expand_first = scatter_about(key_list[4], (C, H), (0.3 * FRAMES ** 0.5), 384.0, ((0, 4), (1, 8)), jnp.float32)
    expand_second = jnp.clip(jnp.exp(math.log(29491.2) - 2.014903 * jax.random.uniform(key_list[5], (C, H), jnp.float32) ** level_of(key_list[5], (C, H), ((0, 4), (1, 8)), -0.2, 0.2)), 3932.16, 29491.2)
    project_weight = scatter_about(key_list[6], (H, C), H ** -0.5, 0.15625, ((0, 8), (1, 4)), jnp.float32)
    project_first = scatter_about(key_list[7], (H, C), (0.5 * FRAMES ** 0.5), 640.0, ((0, 8), (1, 4)), jnp.float32)
    project_second = jnp.clip(jnp.exp(math.log(58982.4) - 1.7917594 * jax.random.uniform(key_list[8], (H, C), jnp.float32) ** level_of(key_list[8], (H, C), ((0, 8), (1, 4)), -0.2, 0.2)), 9830.4, 58982.4)
    hidden_bias = scatter_about(key_list[9], (H,), 0.3, 3.0, ((0, 8),), jnp.float32)
    hidden_bias_first = scatter_about(key_list[10], (H,), (0.3 * FRAMES ** 0.5), 384.0, ((0, 8),), jnp.float32)
    hidden_bias_second = jnp.clip(jnp.exp(math.log(29491.2) - 2.014903 * jax.random.uniform(key_list[11], (H,), jnp.float32) ** level_of(key_list[11], (H,), ((0, 8),), -0.2, 0.2)), 3932.16, 29491.2)
    channel_param = draw_channel_param(jax.random.fold_in(key_list[15], 71), 0)
    channel_first = scatter_about(key_list[13], (12, C), (0.6 * FRAMES ** 0.5), 768.0, ((1, 4),), jnp.float32)
    channel_second = jnp.clip(jnp.exp(math.log(73728.0) - 2.014903 * jax.random.uniform(key_list[14], (12, C), jnp.float32) ** level_of(key_list[14], (12, C), ((1, 4),), -0.2, 0.2)), 9830.4, 73728.0)
    return dict(frames=frames, cotangent=cotangent, lengths=lengths, expand_weight=expand_weight, expand_first=expand_first, expand_second=expand_second, project_weight=project_weight, project_first=project_first, project_second=project_second, hidden_bias=hidden_bias, hidden_bias_first=hidden_bias_first, hidden_bias_second=hidden_bias_second, channel_param=channel_param, channel_first=channel_first, channel_second=channel_second)


@jax.custom_vjp
def low(v):
    return lax.optimization_barrier(v.astype(jnp.bfloat16)).astype(jnp.float32)

@jax.custom_vjp
def low_back(v):
    return v

def low_keep(v):
    return (low(v), None)

def low_pass(kept, grad):
    return (grad,)

def back_keep(v):
    return (v, None)

def back_low(kept, grad):
    return (low(grad),)
low.defvjp(low_keep, low_pass)
low_back.defvjp(back_keep, back_low)
beta_first = 0.5
beta_second = 0.5
adam_eps = 1e-08
decay_rate = 0.01
step_count = 6

def group_forward(params, inputs, lens):
    expand_bf, project_bf, hidden_bias, channel = params
    clips, length, width = inputs.shape
    positions = lax.broadcasted_iota(jnp.int32, (clips, length), 1)
    mask = (positions < lens[:, None]).astype(inputs.dtype)[:, :, None]
    masked = inputs * mask
    padded = jnp.pad(masked, ((0, 0), (3, 3), (0, 0)))
    conv = channel[7] + sum((channel[k] * padded[:, k:k + length] for k in range(7)))
    mean = lax.optimization_barrier(jnp.mean(conv, axis=-1, keepdims=True))
    centered = conv - mean
    var = lax.optimization_barrier(jnp.mean(centered * centered, axis=-1, keepdims=True))
    nhat = centered * lax.rsqrt(var + 1e-06)
    normed = low(nhat * channel[8] + channel[9]).reshape(clips * length, width)
    pre = low_back(jnp.dot(normed, expand_bf, precision=lax.Precision.HIGHEST, preferred_element_type=jnp.float32)) + hidden_bias
    hid = low(jax.nn.gelu(pre, approximate=False))
    branch = low_back(jnp.dot(hid, project_bf, precision=lax.Precision.HIGHEST, preferred_element_type=jnp.float32))
    total = (branch + channel[10]).reshape(clips, length, width)
    return (inputs + channel[11] * total) * mask

def full_forward(expand_weight, project_weight, hidden_bias, channel_param, inputs, lengths):
    params = (low(expand_weight), low(project_weight), hidden_bias, channel_param)
    micro, clips_all, length, width = inputs.shape
    grouped = inputs.reshape(micro * clips_all // CL, CL, length, width)
    lens = lengths.reshape(-1, CL).astype(jnp.int32)
    group_fn = jax.checkpoint(lambda block, counts: group_forward(params, block, counts))

    def advance(carry, item):
        return (carry, group_fn(item[0], item[1]))
    _, outs = lax.scan(advance, None, (grouped, lens))
    return outs.reshape(inputs.shape)

def adam_update(weight, first, second, grad, rate):
    first_new = beta_first * first + (1.0 - beta_first) * grad
    second_new = beta_second * second + (1.0 - beta_second) * grad * grad
    first_hat = first_new / (1.0 - beta_first ** step_count)
    second_hat = second_new / (1.0 - beta_second ** step_count)
    weight_new = weight - rate * (first_hat / (jnp.sqrt(second_hat) + adam_eps) + decay_rate * weight)
    return (weight_new, first_new, second_new)

def reference(frames, cotangent, lengths, expand_weight, expand_first, expand_second, project_weight, project_first, project_second, hidden_bias, hidden_bias_first, hidden_bias_second, channel_param, channel_first, channel_second):
    inputs = frames.astype(jnp.float32)
    back = cotangent.astype(jnp.float32)

    def forward_fn(w_expand, w_project, w_bias, w_channel, x_in):
        return full_forward(w_expand, w_project, w_bias, w_channel, x_in, lengths)
    outputs, pull = jax.vjp(forward_fn, expand_weight, project_weight, hidden_bias, channel_param, inputs)
    g_expand, g_project, g_bias, g_channel, g_inputs = pull(back)
    e_new, e_first, e_second = adam_update(expand_weight, expand_first, expand_second, g_expand, 0.02)
    p_new, p_first, p_second = adam_update(project_weight, project_first, project_second, g_project, 0.01)
    b_new, b_first, b_second = adam_update(hidden_bias, hidden_bias_first, hidden_bias_second, g_bias, 0.1)
    c_new, c_first, c_second = adam_update(channel_param, channel_first, channel_second, g_channel, 0.2)
    return (outputs.astype(jnp.bfloat16), g_inputs.astype(jnp.bfloat16), e_new, e_first, e_second, e_new.astype(jnp.bfloat16), p_new, p_first, p_second, p_new.astype(jnp.bfloat16), b_new, b_first, b_second, c_new, c_first, c_second)
```

```python
import functools
import math

import jax
import jax.numpy as jnp
import numpy as np
from jax import lax
from jax.experimental import pallas as pl
from jax.experimental.pallas import tpu as pltpu
from jax.sharding import PartitionSpec as P

MESH = pl.DeviceIdType.MESH
BF = jnp.bfloat16
F32 = jnp.float32
MIB = 1 << 20

eps_norm = 1e-06
beta_first = 0.5
beta_second = 0.5
adam_eps = 1e-08
decay_rate = 0.01
step_count = 6

ROOT_HALF = math.sqrt(0.5)
LOG2E = math.log2(math.e)
SLOPE_LOG = math.log2(2.0 / math.sqrt(math.pi))

BLOCK = 256
SUB = 16
LANES = 128
HCHUNK = 256
TILE = 16


def adam_update(weight, first, second, grad, rate):
    first_new = beta_first * first + (1.0 - beta_first) * grad
    second_new = beta_second * second + (1.0 - beta_second) * grad * grad
    first_hat = first_new / (1.0 - beta_first**step_count)
    second_hat = second_new / (1.0 - beta_second**step_count)
    weight_new = weight - rate * (
        first_hat / (jnp.sqrt(second_hat) + adam_eps) + decay_rate * weight
    )
    return (weight_new, first_new, second_new)


def gather_kernel(dp_n, t_n, w_ref, b_ref, c_ref, wg_ref, bg_ref, cg_ref, local_sem, ws, wr, bs, br, cs, cr):
    d = lax.axis_index("dp")
    t = lax.axis_index("tensor")
    rows = w_ref.shape[1]

    def piece(dd, tt):
        return wg_ref.at[dd, :, pl.ds(pl.multiple_of(tt * rows, 16), rows), :]

    barrier = pltpu.get_barrier_semaphore()
    for k in range(1, dp_n):
        pl.semaphore_signal(barrier, inc=1, device_id=(lax.rem(d + k, dp_n), t), device_id_type=MESH)
    for k in range(1, t_n):
        pl.semaphore_signal(barrier, inc=1, device_id=(d, jnp.bitwise_xor(t, k)), device_id_type=MESH)
    own_w = pltpu.make_async_copy(w_ref, piece(d, t), local_sem.at[0])
    own_b = pltpu.make_async_copy(b_ref, bg_ref.at[t], local_sem.at[1])
    own_c = pltpu.make_async_copy(c_ref, cg_ref.at[d], local_sem.at[2])
    own_w.start()
    own_b.start()
    own_c.start()
    pl.semaphore_wait(barrier, dp_n - 1 + t_n - 1)

    copies = []

    def send(src, dst, ssem, rsem, peer):
        copy = pltpu.make_async_remote_copy(
            src_ref=src, dst_ref=dst, send_sem=ssem, recv_sem=rsem, device_id=peer, device_id_type=MESH
        )
        copy.start()
        copies.append(copy)

    def arrived(dst, rsem):
        pltpu.make_async_copy(dst, dst, rsem).wait()

    for k in range(1, dp_n):
        peer = (lax.rem(d + k, dp_n), t)
        send(w_ref, piece(d, t), ws.at[0, k], wr.at[d, t], peer)
        send(c_ref, cg_ref.at[d], cs.at[k], cr.at[d], peer)
    for k in range(1, t_n):
        send(b_ref, bg_ref.at[t], bs.at[k], br.at[t], (d, jnp.bitwise_xor(t, k)))
    own_w.wait()
    own_b.wait()
    own_c.wait()
    sib = (d, jnp.bitwise_xor(t, 1))
    near = [jnp.bitwise_xor(t, 2), jnp.bitwise_xor(t, 4)]
    far = jnp.bitwise_xor(t, 6)
    order = [lax.rem(d + k, dp_n) for k in range(dp_n)]
    for k in range(dp_n):
        dd = order[k]
        if k > 0:
            arrived(piece(dd, t), wr.at[dd, t])
        for side in range(2):
            send(piece(dd, t), piece(dd, t), ws.at[1 + side, k], wr.at[dd, t], (d, near[side]))
        send(piece(dd, t), piece(dd, t), ws.at[3, k], wr.at[dd, t], sib)
    half = dp_n // 2
    for k in range(dp_n):
        dd = order[k]
        for side in range(2):
            arrived(piece(dd, near[side]), wr.at[dd, near[side]])
            if (k < half) == (side == 0):
                send(
                    piece(dd, near[side]),
                    piece(dd, near[side]),
                    ws.at[6, k],
                    wr.at[dd, near[side]],
                    (d, near[1 - side]),
                )
            send(piece(dd, near[side]), piece(dd, near[side]), ws.at[4 + side, k], wr.at[dd, near[side]], sib)
    for k in range(dp_n):
        dd = order[k]
        arrived(piece(dd, far), wr.at[dd, far])
        send(piece(dd, far), piece(dd, far), ws.at[7, k], wr.at[dd, far], sib)
    for k in range(dp_n):
        dd = order[k]
        for x in (1, 3, 5, 7):
            tt = jnp.bitwise_xor(t, x)
            arrived(piece(dd, tt), wr.at[dd, tt])
    for k in range(1, dp_n):
        dd = lax.rem(d + k, dp_n)
        arrived(cg_ref.at[dd], cr.at[dd])
    for k in range(1, t_n):
        tt = jnp.bitwise_xor(t, k)
        arrived(bg_ref.at[tt], br.at[tt])
    for copy in copies:
        copy.wait_send()


def gather_weights(dp_n, t_n, w_own, bias, channel):
    two, rows, width = w_own.shape
    return pl.pallas_call(
        functools.partial(gather_kernel, dp_n, t_n),
        out_shape=(
            jax.ShapeDtypeStruct((dp_n, two, rows * t_n, width), w_own.dtype),
            jax.ShapeDtypeStruct((t_n,) + bias.shape, bias.dtype),
            jax.ShapeDtypeStruct((dp_n,) + channel.shape, channel.dtype),
        ),
        in_specs=[pl.BlockSpec(memory_space=pl.ANY)] * 3,
        out_specs=(pl.BlockSpec(memory_space=pl.ANY),) * 3,
        scratch_shapes=[
            pltpu.SemaphoreType.DMA((3,)),
            pltpu.SemaphoreType.DMA((8, dp_n)),
            pltpu.SemaphoreType.DMA((dp_n, t_n)),
            pltpu.SemaphoreType.DMA((t_n,)),
            pltpu.SemaphoreType.DMA((t_n,)),
            pltpu.SemaphoreType.DMA((dp_n,)),
            pltpu.SemaphoreType.DMA((dp_n,)),
        ],
        compiler_params=pltpu.CompilerParams(collective_id=0, has_side_effects=True),
        name="gather_weights",
    )(w_own, bias, channel)


def dot_nn(a, b):
    return lax.dot_general(a, b, (((1,), (0,)), ((), ())), preferred_element_type=F32)


def dot_nt(a, b):
    return lax.dot_general(a, b, (((1,), (1,)), ((), ())), preferred_element_type=F32)


def split_rows(count, largest):
    step = largest
    while step >= TILE:
        yield step, count - lax.rem(count, 2 * step), lax.rem(lax.div(count, step), 2) == 1
        step //= 2


def block_kernel(grads, first, n, base, n_recv, length, width, hidden, *refs):
    refs = list(refs)
    meta, x_hbm, dy_hbm, w_hbm, chan, bias = refs[:6]
    refs = refs[6:]
    if not first:
        refs = refs[2:]
    received = refs[:n_recv]
    refs = refs[n_recv:]
    o_hbm = refs[:2]
    own_hbm = refs[2:4]
    refs = refs[4:]
    if grads:
        g_out, small_out, gbias_out = refs[:3]
        refs = refs[3:]
    (x_pack, dy_pack, ob_pack, gb_pack, w_e, w_p, xs, ds, nh, rs, nrm, dzs, hid, dpre, zero) = refs[:15]
    in_sem, out_sem, w_sem, recv_sem = refs[15:19]
    if grads:
        gacc, left_t, gb_acc, sm_acc = refs[19:23]
    groups = width // LANES
    R = BLOCK

    clip_of = [meta[base + k] for k in range(n)]
    len_of = [meta[8 + base + k] for k in range(n)]
    off = [jnp.int32(0)]
    for k in range(n):
        off.append(off[k] + lax.div(len_of[k] + 3 + TILE - 1, TILE) * TILE)
    tiles_of = [lax.div(len_of[k] + TILE - 1, TILE) * TILE for k in range(n)]
    nblk = lax.div(off[n] + TILE + R - 1, R)

    def aligned(v):
        return pl.multiple_of(v, TILE)

    w_copies = []
    for g in range(groups):
        w_copies.append(pltpu.make_async_copy(w_hbm.at[g, 0], w_e.at[:, pl.ds(g * LANES, LANES)], w_sem.at[0, g]))
        w_copies.append(pltpu.make_async_copy(w_hbm.at[g, 1], w_p.at[:, pl.ds(g * LANES, LANES)], w_sem.at[1, g]))

    def clip_in(k, act):
        for j, (src, dst) in enumerate(((x_hbm, x_pack), (dy_hbm, dy_pack))):
            for p, (size, start, have) in enumerate(split_rows(tiles_of[k], length)):

                @pl.when(have)
                def _():
                    copy = pltpu.make_async_copy(
                        src.at[clip_of[k], pl.ds(aligned(start), size), :],
                        dst.at[pl.ds(aligned(off[k] + start), size), :],
                        in_sem.at[k, j, p],
                    )
                    act(copy)

    def clip_out(k, act):
        for j, (src, dsts) in enumerate(((ob_pack, (o_hbm[0], own_hbm[0])), (gb_pack, (o_hbm[1], own_hbm[1])))):
            shift = TILE * j
            for which, dst in enumerate(dsts):
                view = dst.at[clip_of[k]] if which == 0 else dst.at[k]
                p = 0
                for size, start, have in split_rows(tiles_of[k], length):

                    @pl.when(have)
                    def _():
                        copy = pltpu.make_async_copy(
                            src.at[pl.ds(aligned(off[k] + shift + start), size), :],
                            view.at[pl.ds(aligned(start), size), :],
                            out_sem.at[k, 2 * j + which, p],
                        )
                        act(copy)

                    p += 1
                rest = length - tiles_of[k]
                for size, start, have in split_rows(rest, length // 2):

                    @pl.when(have)
                    def _():
                        copy = pltpu.make_async_copy(
                            zero.at[pl.ds(0, size), :],
                            view.at[pl.ds(aligned(tiles_of[k] + start), size), :],
                            out_sem.at[k, 2 * j + which, p],
                        )
                        act(copy)

                    p += 1

    def recv_copies():
        for k in range(n_recv // 2):
            pass

    row_id = lax.broadcasted_iota(jnp.int32, (TILE, width), 0)

    def clear_tail(ref, k, shift):
        left = lax.rem(len_of[k], TILE)
        at = aligned(off[k] + len_of[k] - left + shift)

        @pl.when(left > 0)
        def _():
            tile = ref[pl.ds(at, TILE), :].astype(F32)
            ref[pl.ds(at, TILE), :] = jnp.where(row_id < left, tile, 0.0).astype(ref.dtype)

    def clear_gap(ref, k):
        clear_tail(ref, k, 0)
        at = aligned(off[k] + tiles_of[k])

        @pl.when(off[k + 1] > at)
        def _():
            ref[pl.ds(at, TILE), :] = jnp.zeros((TILE, width), ref.dtype)

    for k in range(n):
        clip_in(k, lambda c: c.start())
        if k == 0:
            for copy in w_copies:
                copy.start()
    n_each = n_recv // 2
    recv_list = []
    if n_recv:
        rec_n = received[0].shape[0]
        rec_base = base - 3 - rec_n
        for j in range(2):
            for k in range(rec_n):
                recv_list.append(
                    pltpu.make_async_copy(
                        received[j].at[k], o_hbm[j].at[meta[16 + rec_base + k]], recv_sem.at[j, k]
                    )
                )
        for copy in recv_list:
            copy.start()

    zero[...] = jnp.zeros_like(zero)
    tail = R + 2 * TILE
    @pl.loop(0, tail // TILE)
    def _(s):
        at = aligned(off[n] + s * TILE)
        x_pack[pl.ds(at, TILE), :] = jnp.zeros((TILE, width), BF)
        dy_pack[pl.ds(at, TILE), :] = jnp.zeros((TILE, width), BF)

    xs[...] = jnp.zeros_like(xs)
    ds[...] = jnp.zeros_like(ds)
    if grads:
        gacc[...] = jnp.zeros_like(gacc)
        gb_acc[...] = jnp.zeros_like(gb_acc)
        sm_acc[...] = jnp.zeros_like(sm_acc)
    for copy in w_copies:
        copy.wait()

    inv_c = 1.0 / width

    def lane(g):
        return slice(g * LANES, (g + 1) * LANES)

    @pl.loop(0, nblk)
    def _(i):
        top = pl.multiple_of(i * R, R)
        for k in range(n):

            @pl.when(i == lax.div(jnp.maximum(off[k] - TILE, 0), R))
            def _():
                clip_in(k, lambda c: c.wait())
                clear_gap(x_pack, k)
                clear_gap(dy_pack, k)

        @pl.when(i == 0)
        def _():
            for g in range(groups):
                xs[g, pl.ds(R + TILE, TILE), :] = x_pack[pl.ds(0, TILE), lane(g)].astype(F32)

        for g in range(groups):
            xs[g, pl.ds(0, 2 * TILE), :] = xs[g, pl.ds(R, 2 * TILE), :]
            ds[g, pl.ds(0, 2 * TILE), :] = ds[g, pl.ds(R, 2 * TILE), :]
        for s in range(0, R, SUB):
            for g in range(groups):
                xs[g, pl.ds(2 * TILE + s, SUB), :] = x_pack[pl.ds(top + TILE + s, SUB), lane(g)].astype(F32)

        for s in range(0, R, SUB):
            conv = []
            for g in range(groups):
                acc = xs[g, pl.ds(s + 13, SUB), :] * chan[0:1, lane(g)] + chan[7:8, lane(g)]
                for k in range(1, 7):
                    acc = acc + xs[g, pl.ds(s + 13 + k, SUB), :] * chan[k : k + 1, lane(g)]
                conv.append(acc)
            mean = jnp.sum(sum(conv), axis=-1, keepdims=True) * inv_c
            cent = [v - mean for v in conv]
            var = jnp.sum(sum([v * v for v in cent]), axis=-1, keepdims=True) * inv_c
            inv = lax.rsqrt(var + eps_norm)
            rs[pl.ds(s, SUB), :] = jnp.broadcast_to(inv, (SUB, LANES))
            for g in range(groups):
                nhat = cent[g] * inv
                nh[g, pl.ds(s, SUB), :] = nhat
                gain = chan[8:9, lane(g)] * ROOT_HALF
                shift = chan[9:10, lane(g)] * ROOT_HALF
                nrm[pl.ds(s, SUB), lane(g)] = (nhat * gain + shift).astype(BF)
                dzs[pl.ds(s, SUB), lane(g)] = (
                    dy_pack[pl.ds(top + s, SUB), lane(g)].astype(F32) * chan[11:12, lane(g)]
                ).astype(BF)

        for c in range(hidden // HCHUNK):
            cols = slice(c * HCHUNK, (c + 1) * HCHUNK)
            pre = dot_nt(nrm[...], w_e[cols, :])
            dhid = dot_nt(dzs[...], w_p[cols, :])
            add = bias[0:1, cols] * ROOT_HALF
            for s in range(0, R, SUB):
                u = pre[s : s + SUB] + add
                v = 1.0 + lax.erf(u)
                hid[pl.ds(s, SUB), cols] = (u * v).astype(BF)
                e = jnp.exp2(SLOPE_LOG - LOG2E * (u * u))
                dp2 = dhid[s : s + SUB] * (v + u * e)
                dpre[pl.ds(s, SUB), cols] = dp2.astype(BF)
                if grads:
                    gb_acc[:, cols] += dp2[0:8] + dp2[8:16]
        branch = dot_nn(hid[...], w_p[...])
        dn2 = dot_nn(dpre[...], w_e[...])

        for s in range(0, R, SUB):
            dn, prod = [], []
            for g in range(groups):
                br = branch[s : s + SUB, lane(g)]
                scale = chan[11:12, lane(g)]
                x_mid = xs[g, pl.ds(s + TILE, SUB), :]
                ob = x_mid + (br * (scale * ROOT_HALF) + scale * chan[10:11, lane(g)])
                ob_pack[pl.ds(top + s, SUB), lane(g)] = ob.astype(BF)
                d2 = dn2[s : s + SUB, lane(g)]
                nhat = nh[g, pl.ds(s, SUB), :]
                half_gain = chan[8:9, lane(g)] * 0.5
                dn.append(d2 * half_gain)
                if grads:
                    p2 = d2 * nhat
                    prod.append(p2 * half_gain)
                    dyf = dy_pack[pl.ds(top + s, SUB), lane(g)].astype(F32)
                    dyb = dyf * br
                    sm_acc[g, 8] += p2[0:8] + p2[8:16]
                    sm_acc[g, 9] += d2[0:8] + d2[8:16]
                    sm_acc[g, 10] += dyf[0:8] + dyf[8:16]
                    sm_acc[g, 11] += dyb[0:8] + dyb[8:16]
                else:
                    prod.append((d2 * nhat) * half_gain)
            m1 = jnp.sum(sum(dn), axis=-1, keepdims=True) * inv_c
            m2 = jnp.sum(sum(prod), axis=-1, keepdims=True) * inv_c
            inv = rs[pl.ds(s, SUB), :]
            for g in range(groups):
                nhat = nh[g, pl.ds(s, SUB), :]
                dconv = inv * (dn[g] - m1 - nhat * m2)
                ds[g, pl.ds(2 * TILE + s, SUB), :] = dconv
                if grads:
                    sm_acc[g, 7] += dconv[0:8] + dconv[8:16]
                    for k in range(7):
                        tp = dconv * xs[g, pl.ds(s + 13 + k, SUB), :]
                        sm_acc[g, k] += tp[0:8] + tp[8:16]

        for s in range(0, R, SUB):
            for g in range(groups):
                acc = ds[g, pl.ds(s + 19, SUB), :] * chan[0:1, lane(g)]
                for k in range(1, 7):
                    acc = acc + ds[g, pl.ds(s + 19 - k, SUB), :] * chan[k : k + 1, lane(g)]
                if s == 0:
                    back_at = jnp.maximum(top - TILE, 0)
                else:
                    back_at = top + s - TILE
                dyf = dy_pack[pl.ds(aligned(back_at), SUB), lane(g)].astype(F32)
                gb_pack[pl.ds(top + s, SUB), lane(g)] = (dyf + acc).astype(BF)

        if grads:
            for which, (left, right) in enumerate(((nrm, dpre), (dzs, hid))):
                left_t[...] = left[...].T
                for c in range(hidden // HCHUNK):
                    cols = slice(c * HCHUNK, (c + 1) * HCHUNK)
                    gacc[which, :, cols] += dot_nn(left_t[...], right[:, cols])

        for k in range(n):

            @pl.when(i == lax.div(off[k] + len_of[k] + TILE - 1, R))
            def _():
                clear_tail(ob_pack, k, 0)
                clear_tail(gb_pack, k, TILE)
                clip_out(k, lambda c: c.start())

    if grads:
        for which in range(2):
            for c in range(hidden // HCHUNK):
                cols = slice(c * HCHUNK, (c + 1) * HCHUNK)
                g_out[which, cols, :] = (gacc[which, :, cols] * ROOT_HALF).T.astype(BF)
        gbias_out[...] = jnp.sum(gb_acc[...], axis=0, keepdims=True) * 0.5
        for g in range(groups):
            for k in range(12):
                small_out[k : k + 1, lane(g)] = jnp.sum(sm_acc[g, k], axis=0, keepdims=True)
    for k in range(n):
        clip_out(k, lambda c: c.wait())
    for copy in recv_list:
        copy.wait()


def run_block(grads, n, base, meta, x, dy, w, chan, bias, held, received):
    clips, length, width = x.shape
    hidden = w.shape[2]
    groups = width // LANES
    first = held is None
    R = BLOCK
    rows = n * (length + TILE) + 2 * R + 2 * TILE
    out_shape = [jax.ShapeDtypeStruct((clips, length, width), BF)] * 2 + [
        jax.ShapeDtypeStruct((n, length, width), BF)
    ] * 2
    any_spec = pl.BlockSpec(memory_space=pl.ANY)
    vmem_spec = pl.BlockSpec(memory_space=pltpu.VMEM)
    out_specs = [any_spec] * 4
    if grads:
        out_shape += [
            jax.ShapeDtypeStruct((2, hidden, width), BF),
            jax.ShapeDtypeStruct((12, width), F32),
            jax.ShapeDtypeStruct((1, hidden), F32),
        ]
        out_specs += [vmem_spec] * 3
    args = [meta, x, dy, w, chan, bias]
    in_specs = [
        pl.BlockSpec(memory_space=pltpu.SMEM),
        any_spec,
        any_spec,
        any_spec,
        vmem_spec,
        vmem_spec,
    ]
    aliases = {}
    if not first:
        aliases = {6: 0, 7: 1}
        args += list(held)
        in_specs += [any_spec] * 2
    args += list(received)
    in_specs += [any_spec] * len(received)
    scratch = [
        pltpu.VMEM((rows, width), BF),
        pltpu.VMEM((rows, width), BF),
        pltpu.VMEM((rows, width), BF),
        pltpu.VMEM((rows, width), BF),
        pltpu.VMEM((hidden, width), BF),
        pltpu.VMEM((hidden, width), BF),
        pltpu.VMEM((groups, R + 2 * TILE, LANES), F32),
        pltpu.VMEM((groups, R + 2 * TILE, LANES), F32),
        pltpu.VMEM((groups, R, LANES), F32),
        pltpu.VMEM((R, LANES), F32),
        pltpu.VMEM((R, width), BF),
        pltpu.VMEM((R, width), BF),
        pltpu.VMEM((R, hidden), BF),
        pltpu.VMEM((R, hidden), BF),
        pltpu.VMEM((length // 2, width), BF),
        pltpu.SemaphoreType.DMA((n, 2, 8)),
        pltpu.SemaphoreType.DMA((n, 4, 16)),
        pltpu.SemaphoreType.DMA((2, groups)),
        pltpu.SemaphoreType.DMA((2, 8)),
    ]
    if grads:
        scratch += [
            pltpu.VMEM((2, width, hidden), F32),
            pltpu.VMEM((width, R), BF),
            pltpu.VMEM((8, hidden), F32),
            pltpu.VMEM((groups, 12, 8, LANES), F32),
        ]
    per_row = 2 * width * hidden * (6 if grads else 4)
    cost = pl.CostEstimate(
        flops=int(per_row * n * length * 1.5), bytes_accessed=n * length * width * 12, transcendentals=0
    )
    return pl.pallas_call(
        functools.partial(block_kernel, grads, first, n, base, len(received), length, width, hidden),
        out_shape=tuple(out_shape),
        in_specs=in_specs,
        out_specs=tuple(out_specs),
        scratch_shapes=scratch,
        input_output_aliases=aliases,
        cost_estimate=cost,
        compiler_params=pltpu.CompilerParams(vmem_limit_bytes=56 * MIB),
        name="block_grads" if grads else "block_plain",
    )(*args)


def place_kernel(base, counts, meta, *refs):
    n_in = 2 + 2 * len(counts)
    ins = refs[2:n_in]
    outs = refs[n_in : n_in + 2]
    sem = refs[n_in + 2]
    copies = []
    at = base
    for block, count in enumerate(counts):
        for j in range(2):
            for k in range(count):
                copies.append(
                    pltpu.make_async_copy(
                        ins[2 * block + j].at[k], outs[j].at[meta[16 + at + k]], sem.at[j, at - base + k]
                    )
                )
        at += count
    for copy in copies:
        copy.start()
    for copy in copies:
        copy.wait()


def place_received(base, counts, meta, held, arrays):
    any_spec = pl.BlockSpec(memory_space=pl.ANY)
    return pl.pallas_call(
        functools.partial(place_kernel, base, counts),
        out_shape=tuple(jax.ShapeDtypeStruct(h.shape, h.dtype) for h in held),
        in_specs=[pl.BlockSpec(memory_space=pltpu.SMEM)] + [any_spec] * (2 + len(arrays)),
        out_specs=(any_spec,) * 2,
        scratch_shapes=[pltpu.SemaphoreType.DMA((2, sum(counts)))],
        input_output_aliases={1: 0, 2: 1},
        name="place_received",
    )(meta, *held, *arrays)


def swap(value, axis, size, bit):
    return lax.ppermute(value, axis, [(i, i ^ bit) for i in range(size)])


def take_bit(index, bit):
    return lax.rem(lax.div(index, bit), 2)


def halve(value, dim, keep):
    half = value.shape[dim] // 2
    mine = lax.dynamic_slice_in_dim(value, keep * half, half, dim)
    other = lax.dynamic_slice_in_dim(value, (1 - keep) * half, half, dim)
    return mine, other


def fold(value, dim, axis, size, bit):
    keep = take_bit(lax.axis_index(axis), bit)
    mine, other = halve(value, dim, keep)
    got = swap(other, axis, size, bit)
    return (mine.astype(F32) + got.astype(F32)).astype(BF)


def per_device(
    frames,
    cotangent,
    lengths,
    expand_weight,
    expand_first,
    expand_second,
    project_weight,
    project_first,
    project_second,
    hidden_bias,
    hidden_bias_first,
    hidden_bias_second,
    channel_param,
    channel_first,
    channel_second,
    *,
    dp_n,
    t_n,
):
    micro, clips, length, width = frames.shape
    hidden_part = expand_weight.shape[1]
    hidden = hidden_part * t_n
    width_part = expand_weight.shape[0]
    count = micro * clips
    d = lax.axis_index("dp")
    t = lax.axis_index("tensor")

    lens = lengths.reshape(count)
    ids = jnp.arange(count, dtype=jnp.int32)
    ahead = (lens[None, :] > lens[:, None]) | ((lens[None, :] == lens[:, None]) & (ids[None, :] < ids[:, None]))
    rank = jnp.sum(ahead.astype(jnp.int32), axis=1)
    per_core = count // 2
    table = np.zeros((t_n, per_core), np.int32)
    for tt in range(t_n):
        core, chip = tt % 2, tt // 2
        own = [4 * (j // 2) + (3 * (j % 2) if core == 0 else 1 + (j % 2)) for j in range(per_core)]
        pair = [chip, per_core - 1 - chip]
        table[tt] = [own[j] for j in pair] + [own[j] for j in range(per_core) if j not in pair]
    both = np.concatenate([table, table[np.arange(t_n) ^ 1]], axis=1)
    wanted = lax.dynamic_slice_in_dim(jnp.asarray(both), t, 1, 0).reshape(2 * per_core)
    hit = (rank[None, :] == wanted[:, None]).astype(jnp.int32)
    seq = jnp.sum(hit * ids[None, :], axis=1)
    seq_len = jnp.sum(hit * lens[None, :], axis=1)
    meta = jnp.concatenate([seq[:per_core], seq_len[:per_core], seq[per_core:]])

    w_own = jnp.stack([expand_weight.T.astype(BF), project_weight.astype(BF)])
    w_all, bias_all, chan_all = gather_weights(dp_n, t_n, w_own, hidden_bias.reshape(1, hidden_part), channel_param)
    if width_part != LANES:
        w_all = jnp.transpose(w_all, (1, 2, 0, 3)).reshape(2, hidden, width // LANES, LANES)
        w_all = jnp.transpose(w_all, (2, 0, 1, 3))
    bias = bias_all.reshape(1, hidden)
    chan = jnp.transpose(chan_all, (1, 0, 2)).reshape(12, width)

    x = frames.reshape(count, length, width)
    dy = cotangent.reshape(count, length, width)
    calls = [(True, 2), (False, 3), (False, 3)]
    held = None
    base = 0
    pending = []
    for index, (grads, n) in enumerate(calls):
        received = pending[0] if index == 2 else ()
        outs = run_block(grads, n, base, meta, x, dy, w_all, chan, bias, held, received)
        held = outs[:2]
        pending.append(tuple(swap(o, "tensor", t_n, 1) for o in outs[2:4]))
        if grads:
            g_part, small_part, gbias_part = outs[4:]
        base += n
    held = place_received(2, [3, 3], meta, held, pending[1] + pending[2])

    g = g_part.reshape(2, t_n // 2, 2, hidden_part, dp_n, width_part)
    g = jnp.transpose(g, (2, 1, 4, 0, 3, 5)) if False else g
    g = fold(g, 2, "tensor", t_n, 1)
    g = fold(g.reshape(2, 2, 2, hidden_part, dp_n, width_part), 2, "tensor", t_n, 2)
    g = fold(g.reshape(2, 2, hidden_part, dp_n, width_part), 1, "tensor", t_n, 4)
    g = g.reshape(2, hidden_part, dp_n, width_part)
    bit = dp_n // 2
    while bit >= 1:
        g = fold(g, 2, "dp", dp_n, bit)
        bit //= 2
    g = g.reshape(2, hidden_part, width_part).astype(F32)
    shard_expand = g[0].T
    shard_project = g[1]

    small = jnp.concatenate([small_part.reshape(12 * width), gbias_part.reshape(hidden)])
    for bit in (1, 2, 4):
        small = small + swap(small, "tensor", t_n, bit)
    bit = 1
    while bit < dp_n:
        small = small + swap(small, "dp", dp_n, bit)
        bit *= 2
    g_small = lax.dynamic_slice_in_dim(small[: 12 * width].reshape(12, width), d * width_part, width_part, 1)
    g_bias = lax.dynamic_slice_in_dim(small[12 * width :], t * hidden_part, hidden_part, 0)
    back_sum = g_small[10]
    shard_channel = jnp.concatenate(
        [
            g_small[0:8],
            g_small[8:10] * 0.5,
            (back_sum * channel_param[11])[None],
            (g_small[11] * ROOT_HALF + back_sum * channel_param[10])[None],
        ],
        axis=0,
    )

    e_new, e_first, e_second = adam_update(expand_weight, expand_first, expand_second, shard_expand, 0.02)
    p_new, p_first, p_second = adam_update(project_weight, project_first, project_second, shard_project, 0.01)
    b_new, b_first, b_second = adam_update(hidden_bias, hidden_bias_first, hidden_bias_second, g_bias, 0.1)
    c_new, c_first, c_second = adam_update(channel_param, channel_first, channel_second, shard_channel, 0.2)
    return (
        held[0].reshape(frames.shape),
        held[1].reshape(frames.shape),
        e_new,
        e_first,
        e_second,
        e_new.astype(BF),
        p_new,
        p_first,
        p_second,
        p_new.astype(BF),
        b_new,
        b_first,
        b_second,
        c_new,
        c_first,
        c_second,
    )


def solution(mesh):
    frame_spec = P(None, "dp", None, None)
    e_spec = P("dp", "tensor")
    p_spec = P("tensor", "dp")
    b_spec = P("tensor")
    c_spec = P(None, "dp")
    in_specs = (
        (frame_spec, frame_spec, P(None, "dp")) + (e_spec,) * 3 + (p_spec,) * 3 + (b_spec,) * 3 + (c_spec,) * 3
    )
    out_specs = (frame_spec, frame_spec) + (e_spec,) * 4 + (p_spec,) * 4 + (b_spec,) * 3 + (c_spec,) * 3
    body = functools.partial(per_device, dp_n=mesh.shape["dp"], t_n=mesh.shape["tensor"])
    return jax.shard_map(body, mesh=mesh, in_specs=in_specs, out_specs=out_specs, check_vma=False)
```

```python
import functools
import math

import jax
import jax.numpy as jnp
import numpy as np
from jax import lax
from jax.experimental import pallas as pl
from jax.experimental.pallas import tpu as pltpu
from jax.sharding import PartitionSpec as P

MESH = pl.DeviceIdType.MESH
BF = jnp.bfloat16
F32 = jnp.float32
MIB = 1 << 20

eps_norm = 1e-06
beta_first = 0.5
beta_second = 0.5
adam_eps = 1e-08
decay_rate = 0.01
step_count = 6

ROOT_HALF = math.sqrt(0.5)
LOG2E = math.log2(math.e)
SLOPE_LOG = math.log2(2.0 / math.sqrt(math.pi))

BLOCK = 512
SUB = 16
LANES = 128
HCHUNK = 256
TILE = 16


def adam_update(weight, first, second, grad, rate):
    first_new = beta_first * first + (1.0 - beta_first) * grad
    second_new = beta_second * second + (1.0 - beta_second) * grad * grad
    first_hat = first_new / (1.0 - beta_first**step_count)
    second_hat = second_new / (1.0 - beta_second**step_count)
    weight_new = weight - rate * (
        first_hat / (jnp.sqrt(second_hat) + adam_eps) + decay_rate * weight
    )
    return (weight_new, first_new, second_new)


def gather_kernel(dp_n, t_n, w_ref, b_ref, c_ref, wg_ref, bg_ref, cg_ref, local_sem, ws, wr, bs, br, cs, cr):
    d = lax.axis_index("dp")
    t = lax.axis_index("tensor")
    rows = w_ref.shape[1]

    def piece(dd, tt):
        return wg_ref.at[dd, :, pl.ds(pl.multiple_of(tt * rows, 16), rows), :]

    barrier = pltpu.get_barrier_semaphore()
    for k in range(1, dp_n):
        pl.semaphore_signal(barrier, inc=1, device_id=(lax.rem(d + k, dp_n), t), device_id_type=MESH)
    for k in range(1, t_n):
        pl.semaphore_signal(barrier, inc=1, device_id=(d, jnp.bitwise_xor(t, k)), device_id_type=MESH)
    own_w = pltpu.make_async_copy(w_ref, piece(d, t), local_sem.at[0])
    own_b = pltpu.make_async_copy(b_ref, bg_ref.at[t], local_sem.at[1])
    own_c = pltpu.make_async_copy(c_ref, cg_ref.at[d], local_sem.at[2])
    own_w.start()
    own_b.start()
    own_c.start()
    pl.semaphore_wait(barrier, dp_n - 1 + t_n - 1)

    copies = []

    def send(src, dst, ssem, rsem, peer):
        copy = pltpu.make_async_remote_copy(
            src_ref=src, dst_ref=dst, send_sem=ssem, recv_sem=rsem, device_id=peer, device_id_type=MESH
        )
        copy.start()
        copies.append(copy)

    def arrived(dst, rsem):
        pltpu.make_async_copy(dst, dst, rsem).wait()

    for k in range(1, dp_n):
        peer = (lax.rem(d + k, dp_n), t)
        send(w_ref, piece(d, t), ws.at[0, k], wr.at[d, t], peer)
        send(c_ref, cg_ref.at[d], cs.at[k], cr.at[d], peer)
    for k in range(1, t_n):
        send(b_ref, bg_ref.at[t], bs.at[k], br.at[t], (d, jnp.bitwise_xor(t, k)))
    own_w.wait()
    own_b.wait()
    own_c.wait()
    sib = (d, jnp.bitwise_xor(t, 1))
    near = [jnp.bitwise_xor(t, 2), jnp.bitwise_xor(t, 4)]
    far = jnp.bitwise_xor(t, 6)
    order = [lax.rem(d + k, dp_n) for k in range(dp_n)]
    for k in range(dp_n):
        dd = order[k]
        if k > 0:
            arrived(piece(dd, t), wr.at[dd, t])
        for side in range(2):
            send(piece(dd, t), piece(dd, t), ws.at[1 + side, k], wr.at[dd, t], (d, near[side]))
        send(piece(dd, t), piece(dd, t), ws.at[3, k], wr.at[dd, t], sib)
    half = dp_n // 2
    for k in range(dp_n):
        dd = order[k]
        for side in range(2):
            arrived(piece(dd, near[side]), wr.at[dd, near[side]])
            if (k < half) == (side == 0):
                send(
                    piece(dd, near[side]),
                    piece(dd, near[side]),
                    ws.at[6, k],
                    wr.at[dd, near[side]],
                    (d, near[1 - side]),
                )
            send(piece(dd, near[side]), piece(dd, near[side]), ws.at[4 + side, k], wr.at[dd, near[side]], sib)
    for k in range(dp_n):
        dd = order[k]
        arrived(piece(dd, far), wr.at[dd, far])
        send(piece(dd, far), piece(dd, far), ws.at[7, k], wr.at[dd, far], sib)
    for k in range(dp_n):
        dd = order[k]
        for x in (1, 3, 5, 7):
            tt = jnp.bitwise_xor(t, x)
            arrived(piece(dd, tt), wr.at[dd, tt])
    for k in range(1, dp_n):
        dd = lax.rem(d + k, dp_n)
        arrived(cg_ref.at[dd], cr.at[dd])
    for k in range(1, t_n):
        tt = jnp.bitwise_xor(t, k)
        arrived(bg_ref.at[tt], br.at[tt])
    for copy in copies:
        copy.wait_send()


def gather_weights(dp_n, t_n, w_own, bias, channel):
    two, rows, width = w_own.shape
    return pl.pallas_call(
        functools.partial(gather_kernel, dp_n, t_n),
        out_shape=(
            jax.ShapeDtypeStruct((dp_n, two, rows * t_n, width), w_own.dtype),
            jax.ShapeDtypeStruct((t_n,) + bias.shape, bias.dtype),
            jax.ShapeDtypeStruct((dp_n,) + channel.shape, channel.dtype),
        ),
        in_specs=[pl.BlockSpec(memory_space=pl.ANY)] * 3,
        out_specs=(pl.BlockSpec(memory_space=pl.ANY),) * 3,
        scratch_shapes=[
            pltpu.SemaphoreType.DMA((3,)),
            pltpu.SemaphoreType.DMA((8, dp_n)),
            pltpu.SemaphoreType.DMA((dp_n, t_n)),
            pltpu.SemaphoreType.DMA((t_n,)),
            pltpu.SemaphoreType.DMA((t_n,)),
            pltpu.SemaphoreType.DMA((dp_n,)),
            pltpu.SemaphoreType.DMA((dp_n,)),
        ],
        compiler_params=pltpu.CompilerParams(collective_id=0, has_side_effects=True),
        name="gather_weights",
    )(w_own, bias, channel)


def dot_nn(a, b):
    return lax.dot_general(a, b, (((1,), (0,)), ((), ())), preferred_element_type=F32)


def dot_nt(a, b):
    return lax.dot_general(a, b, (((1,), (1,)), ((), ())), preferred_element_type=F32)


def split_rows(count, largest):
    step = largest
    while step >= TILE:
        yield step, count - lax.rem(count, 2 * step), lax.rem(lax.div(count, step), 2) == 1
        step //= 2


def block_kernel(grads, first, n, base, n_recv, rec_base, length, width, hidden, *refs):
    refs = list(refs)
    meta, x_hbm, dy_hbm, w_hbm, chan, bias = refs[:6]
    refs = refs[6:]
    if not first:
        refs = refs[2:]
    received = refs[:n_recv]
    refs = refs[n_recv:]
    o_hbm = refs[:2]
    own_hbm = refs[2:4]
    refs = refs[4:]
    if grads:
        g_out, small_out, gbias_out = refs[:3]
        refs = refs[3:]
    (x_pack, dy_pack, ob_pack, gb_pack, w_e, w_p) = refs[:6]
    xs, nh, rs, ds, nrm, dzs, br, dn2, hid, dpre, pre_s, dh_s, pc, pb, zero = refs[6:21]
    in_sem, out_sem, w_sem = refs[21:24]
    refs = refs[24:]
    if n_recv:
        stage, recv_sem = refs[:2]
        refs = refs[2:]
    if grads:
        gacc, left_t, gb_acc, sm_acc = refs
    groups = width // LANES
    R = BLOCK

    clip_of = [meta[base + k] for k in range(n)]
    len_of = [meta[8 + base + k] for k in range(n)]
    off = [jnp.int32(0)]
    for k in range(n):
        off.append(off[k] + lax.div(len_of[k] + 3 + TILE - 1, TILE) * TILE)
    tiles_of = [lax.div(len_of[k] + TILE - 1, TILE) * TILE for k in range(n)]
    nblk = lax.div(off[n] + TILE + R - 1, R)
    x_lead, dy_lead, ob_lead, gb_lead = TILE, R + TILE, R, R + TILE

    def aligned(v):
        return pl.multiple_of(v, TILE)

    w_copies = []
    for g in range(groups):
        w_copies.append(pltpu.make_async_copy(w_hbm.at[g, 0], w_e.at[:, pl.ds(g * LANES, LANES)], w_sem.at[0, g]))
        w_copies.append(pltpu.make_async_copy(w_hbm.at[g, 1], w_p.at[:, pl.ds(g * LANES, LANES)], w_sem.at[1, g]))

    def clip_in(k, act):
        for j, (src, dst, lead) in enumerate(((x_hbm, x_pack, x_lead), (dy_hbm, dy_pack, dy_lead))):
            for p, (size, start, have) in enumerate(split_rows(tiles_of[k], length)):

                @pl.when(have)
                def _():
                    copy = pltpu.make_async_copy(
                        src.at[clip_of[k], pl.ds(aligned(start), size), :],
                        dst.at[pl.ds(aligned(off[k] + lead + start), size), :],
                        in_sem.at[k, j, p],
                    )
                    act(copy)

    def clip_out(k, act):
        for j, (src, lead) in enumerate(((ob_pack, ob_lead), (gb_pack, gb_lead))):
            for which, dst in enumerate((o_hbm[j], own_hbm[j])):
                view = dst.at[clip_of[k]] if which == 0 else dst.at[k]
                p = 0
                for size, start, have in split_rows(tiles_of[k], length):

                    @pl.when(have)
                    def _():
                        copy = pltpu.make_async_copy(
                            src.at[pl.ds(aligned(off[k] + lead + start), size), :],
                            view.at[pl.ds(aligned(start), size), :],
                            out_sem.at[k, 2 * j + which, p],
                        )
                        act(copy)

                    p += 1
                rest = length - tiles_of[k]
                for size, start, have in split_rows(rest, length // 2):

                    @pl.when(have)
                    def _():
                        copy = pltpu.make_async_copy(
                            zero.at[pl.ds(0, size), :],
                            view.at[pl.ds(aligned(tiles_of[k] + start), size), :],
                            out_sem.at[k, 2 * j + which, p],
                        )
                        act(copy)

                    p += 1

    row_id = lax.broadcasted_iota(jnp.int32, (TILE, width), 0)

    def clear_tail(ref, k, lead):
        left = lax.rem(len_of[k], TILE)
        at = aligned(off[k] + len_of[k] - left + lead)

        @pl.when(left > 0)
        def _():
            tile = ref[pl.ds(at, TILE), :].astype(F32)
            ref[pl.ds(at, TILE), :] = jnp.where(row_id < left, tile, 0.0).astype(ref.dtype)

    def clear_gap(ref, k, lead):
        clear_tail(ref, k, lead)
        at = aligned(off[k] + tiles_of[k] + lead)

        @pl.when(off[k + 1] > off[k] + tiles_of[k])
        def _():
            ref[pl.ds(at, TILE), :] = jnp.zeros((TILE, width), ref.dtype)

    def clip_ready(k):
        clip_in(k, lambda c: c.wait())
        clear_gap(x_pack, k, x_lead)
        clear_gap(dy_pack, k, dy_lead)

    def clip_done(k):
        clear_tail(ob_pack, k, ob_lead)
        clear_tail(gb_pack, k, gb_lead)
        clip_out(k, lambda c: c.start())

    for k in range(n):
        clip_in(k, lambda c: c.start())
        if k == 0:
            for copy in w_copies:
                copy.start()
    recv_in, recv_out = [], []
    if n_recv:
        rec_n = received[0].shape[0]
        for j in range(2):
            for k in range(rec_n):
                recv_in.append(pltpu.make_async_copy(received[j].at[k], stage.at[j, k], recv_sem.at[0, j, k]))
                recv_out.append(
                    pltpu.make_async_copy(stage.at[j, k], o_hbm[j].at[meta[16 + rec_base + k]], recv_sem.at[1, j, k])
                )
        for copy in recv_in:
            copy.start()

    zero[...] = jnp.zeros_like(zero)
    x_pack[pl.ds(0, x_lead), :] = jnp.zeros((x_lead, width), BF)
    dy_pack[pl.ds(0, dy_lead), :] = jnp.zeros((dy_lead, width), BF)

    @pl.loop(0, (R + 4 * TILE) // TILE)
    def _(s):
        at = off[n] + s * TILE
        x_pack[pl.ds(aligned(at + x_lead), TILE), :] = jnp.zeros((TILE, width), BF)
        dy_pack[pl.ds(aligned(at + dy_lead), TILE), :] = jnp.zeros((TILE, width), BF)

    for ref in (xs, nh, rs, br, dn2, ds):
        ref[...] = jnp.zeros_like(ref)
    if grads:
        gacc[...] = jnp.zeros_like(gacc)
        gb_acc[...] = jnp.zeros_like(gb_acc)
        sm_acc[...] = jnp.zeros_like(sm_acc)
    scale = chan[11:12, :]
    pc[0:8, :] = chan[0:8, :]
    pc[8:10, :] = chan[8:10, :] * ROOT_HALF
    pc[10:11, :] = scale * chan[10:11, :]
    pc[11:12, :] = scale
    pc[12:13, :] = scale * ROOT_HALF
    pc[13:14, :] = chan[8:9, :] * 0.5
    pb[...] = bias[...] * ROOT_HALF

    inv_c = 1.0 / width

    def lane(g):
        return slice(g * LANES, (g + 1) * LANES)

    def row(r, g):
        return pc[r : r + 1, lane(g)]

    def conv_tasks(b, q):
        top = b * R

        def ingest(s):
            for g in range(groups):
                xs[q, g, pl.ds(s, SUB), :] = x_pack[pl.ds(aligned(top + s), SUB), lane(g)].astype(F32)

        def conv_norm(s):
            conv = []
            for g in range(groups):
                acc = xs[q, g, pl.ds(s + 13, SUB), :] * row(0, g) + row(7, g)
                for k in range(1, 7):
                    acc = acc + xs[q, g, pl.ds(s + 13 + k, SUB), :] * row(k, g)
                conv.append(acc)
            mean = jnp.sum(sum(conv), axis=-1, keepdims=True) * inv_c
            cent = [v - mean for v in conv]
            var = jnp.sum(sum([v * v for v in cent]), axis=-1, keepdims=True) * inv_c
            inv = lax.rsqrt(var + eps_norm)
            rs[q, pl.ds(s, SUB), :] = jnp.broadcast_to(inv, (SUB, LANES))
            for g in range(groups):
                nhat = cent[g] * inv
                nh[q, g, pl.ds(s, SUB), :] = nhat
                nrm[pl.ds(s, SUB), lane(g)] = (nhat * row(8, g) + row(9, g)).astype(BF)
                dyf = dy_pack[pl.ds(aligned(top + dy_lead + s), SUB), lane(g)].astype(F32)
                dzs[pl.ds(s, SUB), lane(g)] = (dyf * row(11, g)).astype(BF)

        tasks = []
        lead = 2 * TILE
        for s in range(0, lead, SUB):
            tasks.append(functools.partial(ingest, s))
        for s in range(0, R, SUB):
            tasks.append(functools.partial(ingest, s + lead))
            tasks.append(functools.partial(conv_norm, s))
        return tasks

    def post_tasks(b, q):
        top = b * R

        def norm_back(s):
            dn, prod = [], []
            for g in range(groups):
                bv = br[pl.ds(s, SUB), lane(g)]
                x_mid = xs[q, g, pl.ds(s + TILE, SUB), :]
                ob = (x_mid + row(10, g)) + bv * row(12, g)
                ob_pack[pl.ds(aligned(top + ob_lead + s), SUB), lane(g)] = ob.astype(BF)
                d2 = dn2[pl.ds(s, SUB), lane(g)]
                nhat = nh[q, g, pl.ds(s, SUB), :]
                dg = d2 * row(13, g)
                dn.append(dg)
                prod.append(dg * nhat)
                if grads:
                    p2 = d2 * nhat
                    dyf = dy_pack[pl.ds(aligned(top + dy_lead + s), SUB), lane(g)].astype(F32)
                    dyb = dyf * bv
                    sm_acc[g, 8] += p2[0:8] + p2[8:16]
                    sm_acc[g, 9] += d2[0:8] + d2[8:16]
                    sm_acc[g, 10] += dyf[0:8] + dyf[8:16]
                    sm_acc[g, 11] += dyb[0:8] + dyb[8:16]
            m1 = jnp.sum(sum(dn), axis=-1, keepdims=True) * inv_c
            m2 = jnp.sum(sum(prod), axis=-1, keepdims=True) * inv_c
            inv = rs[q, pl.ds(s, SUB), :]
            for g in range(groups):
                nhat = nh[q, g, pl.ds(s, SUB), :]
                dconv = inv * (dn[g] - m1 - nhat * m2)
                ds[g, pl.ds(2 * TILE + s, SUB), :] = dconv
                if grads:
                    sm_acc[g, 7] += dconv[0:8] + dconv[8:16]
                    for k in range(7):
                        tp = dconv * xs[q, g, pl.ds(s + 13 + k, SUB), :]
                        sm_acc[g, k] += tp[0:8] + tp[8:16]

        def carry():
            for g in range(groups):
                ds[g, pl.ds(0, 2 * TILE), :] = ds[g, pl.ds(R, 2 * TILE), :]

        return [carry] + [functools.partial(norm_back, s) for s in range(0, R, SUB)]

    def frame_tasks(b):
        top = b * R

        def frames_back(s):
            for g in range(groups):
                acc = dy_pack[pl.ds(aligned(top + R + s), SUB), lane(g)].astype(F32)
                for k in range(7):
                    acc = acc + ds[g, pl.ds(s + 19 - k, SUB), :] * row(k, g)
                gb_pack[pl.ds(aligned(top + R + s), SUB), lane(g)] = acc.astype(BF)

        return [functools.partial(frames_back, s) for s in range(0, R, SUB)]

    def up_step(c):
        cols = slice(c * HCHUNK, (c + 1) * HCHUNK)

        def one():
            pre_s[c % 2] = dot_nt(nrm[...], w_e[cols, :])

        def two():
            dh_s[c % 2] = dot_nt(dzs[...], w_p[cols, :])

        return [one, two]

    def gelu_tasks(c):
        cols = slice(c * HCHUNK, (c + 1) * HCHUNK)

        def part(s):
            u = pre_s[c % 2, pl.ds(s, SUB), :] + pb[0:1, cols]
            v = 1.0 + lax.erf(u)
            hid[pl.ds(s, SUB), cols] = (u * v).astype(BF)
            e = jnp.exp2(SLOPE_LOG - LOG2E * (u * u))
            dp2 = dh_s[c % 2, pl.ds(s, SUB), :] * (v + u * e)
            dpre[pl.ds(s, SUB), cols] = dp2.astype(BF)
            if grads:
                gb_acc[:, cols] += dp2[0:8] + dp2[8:16]

        return [functools.partial(part, s) for s in range(0, R, SUB)]

    def down_steps():
        steps = []
        for h in range(2):
            cols = slice(h * (width // 2), (h + 1) * (width // 2))

            def one(cols=cols):
                br[:, cols] = dot_nn(hid[...], w_p[:, cols])

            def two(cols=cols):
                dn2[:, cols] = dot_nn(dpre[...], w_e[:, cols])

            steps += [one, two]
        return steps

    def grad_steps():
        steps = []

        def turn():
            left_t[0] = nrm[...].T
            left_t[1] = dzs[...].T

        for c in range(hidden // HCHUNK):
            cols = slice(c * HCHUNK, (c + 1) * HCHUNK)
            for which, right in enumerate((dpre, hid)):

                def step(which=which, right=right, cols=cols):
                    gacc[which, :, cols] += dot_nn(left_t[which], right[:, cols])

                steps.append(step)
        return turn, steps

    def interleave(steps, tasks):
        done = 0
        for index, step in enumerate(steps):
            step()
            upto = len(tasks) * (index + 1) // len(steps)
            while done < upto:
                tasks[done]()
                done += 1

    def merge(first_list, second_list):
        total = [(index / len(part), which, task) for which, part in enumerate((first_list, second_list)) for index, task in enumerate(part)]
        return [task for _, _, task in sorted(total, key=lambda item: item[:2])]

    def run_tasks(tasks):
        for task in tasks:
            task()

    for k in range(n):

        @pl.when(off[k] < R + TILE)
        def _():
            clip_ready(k)

    run_tasks(conv_tasks(0, 0))
    for copy in w_copies:
        copy.wait()
    n_chunk = hidden // HCHUNK

    @pl.loop(0, nblk)
    def _(i):
        q = lax.rem(i, 2)
        for k in range(n):

            @pl.when((off[k] >= (i + 1) * R + TILE) & (off[k] < (i + 2) * R + TILE))
            def _():
                clip_ready(k)

        post = post_tasks(i - 1, 1 - q)
        for c in range(n_chunk):
            mine = post[len(post) * c // n_chunk : len(post) * (c + 1) // n_chunk]
            interleave(up_step(c), merge(gelu_tasks(c - 1), mine) if c else mine)
        run_tasks(gelu_tasks(n_chunk - 1))
        rest = merge(conv_tasks(i + 1, 1 - q), frame_tasks(i - 1))
        if grads:
            turn, steps = grad_steps()
            turn()
            interleave(down_steps() + steps, rest)
        else:
            interleave(down_steps(), rest)

        if n_recv:

            @pl.when(i == 0)
            def _():
                for copy in recv_in:
                    copy.wait()
                for copy in recv_out:
                    copy.start()

        for k in range(n):
            end = off[k] + len_of[k] + TILE

            @pl.when((end > (i - 1) * R) & (end <= i * R))
            def _():
                clip_done(k)

    run_tasks(post_tasks(nblk - 1, lax.rem(nblk - 1, 2)))
    run_tasks(frame_tasks(nblk - 1))
    for k in range(n):

        @pl.when(off[k] + len_of[k] + TILE > (nblk - 1) * R)
        def _():
            clip_done(k)

    if grads:
        for which in range(2):
            for c in range(hidden // HCHUNK):
                cols = slice(c * HCHUNK, (c + 1) * HCHUNK)
                g_out[which, cols, :] = (gacc[which, :, cols] * ROOT_HALF).T.astype(BF)
        gbias_out[...] = jnp.sum(gb_acc[...], axis=0, keepdims=True) * 0.5
        for g in range(groups):
            for k in range(12):
                small_out[k : k + 1, lane(g)] = jnp.sum(sm_acc[g, k], axis=0, keepdims=True)
    for k in range(n):
        clip_out(k, lambda c: c.wait())
    for copy in recv_out:
        copy.wait()


def run_block(grads, n, base, meta, x, dy, w, chan, bias, held, received, rec_base=0):
    clips, length, width = x.shape
    hidden = w.shape[2]
    groups = width // LANES
    first = held is None
    R = BLOCK
    rows = n * (length + TILE) + 3 * R + 8 * TILE
    out_shape = [jax.ShapeDtypeStruct((clips, length, width), BF)] * 2 + [
        jax.ShapeDtypeStruct((n, length, width), BF)
    ] * 2
    any_spec = pl.BlockSpec(memory_space=pl.ANY)
    vmem_spec = pl.BlockSpec(memory_space=pltpu.VMEM)
    out_specs = [any_spec] * 4
    if grads:
        out_shape += [
            jax.ShapeDtypeStruct((2, hidden, width), BF),
            jax.ShapeDtypeStruct((12, width), F32),
            jax.ShapeDtypeStruct((1, hidden), F32),
        ]
        out_specs += [vmem_spec] * 3
    args = [meta, x, dy, w, chan, bias]
    in_specs = [
        pl.BlockSpec(memory_space=pltpu.SMEM),
        any_spec,
        any_spec,
        any_spec,
        vmem_spec,
        vmem_spec,
    ]
    aliases = {}
    if not first:
        aliases = {6: 0, 7: 1}
        args += list(held)
        in_specs += [any_spec] * 2
    args += list(received)
    in_specs += [any_spec] * len(received)
    scratch = [pltpu.VMEM((rows, width), BF)] * 4 + [pltpu.VMEM((hidden, width), BF)] * 2
    scratch += [
        pltpu.VMEM((2, groups, R + 2 * TILE, LANES), F32),
        pltpu.VMEM((2, groups, R, LANES), F32),
        pltpu.VMEM((2, R, LANES), F32),
        pltpu.VMEM((groups, R + 2 * TILE, LANES), F32),
    ]
    scratch += [pltpu.VMEM((R, width), BF)] * 2
    scratch += [pltpu.VMEM((R, width), F32)] * 2
    scratch += [pltpu.VMEM((R, hidden), BF)] * 2
    scratch += [pltpu.VMEM((2, R, HCHUNK), F32)] * 2
    scratch += [
        pltpu.VMEM((16, width), F32),
        pltpu.VMEM((1, hidden), F32),
        pltpu.VMEM((length // 2, width), BF),
        pltpu.SemaphoreType.DMA((n, 2, 8)),
        pltpu.SemaphoreType.DMA((n, 4, 16)),
        pltpu.SemaphoreType.DMA((2, groups)),
    ]
    if received:
        rec_n = received[0].shape[0]
        scratch += [pltpu.VMEM((2, rec_n, length, width), BF), pltpu.SemaphoreType.DMA((2, 2, rec_n))]
    if grads:
        scratch += [
            pltpu.VMEM((2, width, hidden), F32),
            pltpu.VMEM((2, width, R), BF),
            pltpu.VMEM((8, hidden), F32),
            pltpu.VMEM((groups, 12, 8, LANES), F32),
        ]
    per_row = 2 * width * hidden * (6 if grads else 4)
    cost = pl.CostEstimate(
        flops=int(per_row * n * length * 1.5), bytes_accessed=n * length * width * 12, transcendentals=0
    )
    return pl.pallas_call(
        functools.partial(block_kernel, grads, first, n, base, len(received), rec_base, length, width, hidden),
        out_shape=tuple(out_shape),
        in_specs=in_specs,
        out_specs=tuple(out_specs),
        scratch_shapes=scratch,
        input_output_aliases=aliases,
        cost_estimate=cost,
        compiler_params=pltpu.CompilerParams(vmem_limit_bytes=56 * MIB),
        name="block_grads" if grads else "block_plain",
    )(*args)


def place_kernel(base, counts, meta, *refs):
    n_in = 2 + 2 * len(counts)
    ins = refs[2:n_in]
    outs = refs[n_in : n_in + 2]
    stage, sem = refs[n_in + 2 :]
    taken, placed = [], []
    at = 0
    for block, count in enumerate(counts):
        for k in range(count):
            for j in range(2):
                taken.append(pltpu.make_async_copy(ins[2 * block + j].at[k], stage.at[j, at], sem.at[0, j, at]))
                placed.append(
                    pltpu.make_async_copy(stage.at[j, at], outs[j].at[meta[16 + base + at]], sem.at[1, j, at])
                )
            at += 1
    for copy in taken:
        copy.start()
    for one, two in zip(taken, placed):
        one.wait()
        two.start()
    for copy in placed:
        copy.wait()


def place_received(base, counts, meta, held, arrays):
    any_spec = pl.BlockSpec(memory_space=pl.ANY)
    length, width = held[0].shape[1:]
    total = sum(counts)
    return pl.pallas_call(
        functools.partial(place_kernel, base, counts),
        out_shape=tuple(jax.ShapeDtypeStruct(h.shape, h.dtype) for h in held),
        in_specs=[pl.BlockSpec(memory_space=pltpu.SMEM)] + [any_spec] * (2 + len(arrays)),
        out_specs=(any_spec,) * 2,
        scratch_shapes=[pltpu.VMEM((2, total, length, width), BF), pltpu.SemaphoreType.DMA((2, 2, total))],
        input_output_aliases={1: 0, 2: 1},
        compiler_params=pltpu.CompilerParams(vmem_limit_bytes=40 * MIB),
        name="place_received",
    )(meta, *held, *arrays)


def swap(value, axis, size, bit):
    return lax.ppermute(value, axis, [(i, i ^ bit) for i in range(size)])


def take_bit(index, bit):
    return lax.rem(lax.div(index, bit), 2)


def halve(value, dim, keep):
    half = value.shape[dim] // 2
    mine = lax.dynamic_slice_in_dim(value, keep * half, half, dim)
    other = lax.dynamic_slice_in_dim(value, (1 - keep) * half, half, dim)
    return mine, other


def fold(value, dim, axis, size, bit):
    keep = take_bit(lax.axis_index(axis), bit)
    mine, other = halve(value, dim, keep)
    got = swap(other, axis, size, bit)
    return (mine.astype(F32) + got.astype(F32)).astype(BF)


def per_device(
    frames,
    cotangent,
    lengths,
    expand_weight,
    expand_first,
    expand_second,
    project_weight,
    project_first,
    project_second,
    hidden_bias,
    hidden_bias_first,
    hidden_bias_second,
    channel_param,
    channel_first,
    channel_second,
    *,
    dp_n,
    t_n,
):
    micro, clips, length, width = frames.shape
    hidden_part = expand_weight.shape[1]
    hidden = hidden_part * t_n
    width_part = expand_weight.shape[0]
    count = micro * clips
    d = lax.axis_index("dp")
    t = lax.axis_index("tensor")

    lens = lengths.reshape(count)
    ids = jnp.arange(count, dtype=jnp.int32)
    ahead = (lens[None, :] > lens[:, None]) | ((lens[None, :] == lens[:, None]) & (ids[None, :] < ids[:, None]))
    rank = jnp.sum(ahead.astype(jnp.int32), axis=1)
    per_core = count // 2
    table = np.zeros((t_n, per_core), np.int32)
    for tt in range(t_n):
        core, chip = tt % 2, tt // 2
        own = [4 * (j // 2) + (3 * (j % 2) if core == 0 else 1 + (j % 2)) for j in range(per_core)]
        pair = [chip, per_core - 1 - chip]
        table[tt] = [own[j] for j in pair] + [own[j] for j in range(per_core) if j not in pair]
    both = np.concatenate([table, table[np.arange(t_n) ^ 1]], axis=1)
    wanted = lax.dynamic_slice_in_dim(jnp.asarray(both), t, 1, 0).reshape(2 * per_core)
    hit = (rank[None, :] == wanted[:, None]).astype(jnp.int32)
    seq = jnp.sum(hit * ids[None, :], axis=1)
    seq_len = jnp.sum(hit * lens[None, :], axis=1)
    meta = jnp.concatenate([seq[:per_core], seq_len[:per_core], seq[per_core:]])

    w_own = jnp.stack([expand_weight.T.astype(BF), project_weight.astype(BF)])
    w_all, bias_all, chan_all = gather_weights(dp_n, t_n, w_own, hidden_bias.reshape(1, hidden_part), channel_param)
    if width_part != LANES:
        w_all = jnp.transpose(w_all, (1, 2, 0, 3)).reshape(2, hidden, width // LANES, LANES)
        w_all = jnp.transpose(w_all, (2, 0, 1, 3))
    bias = bias_all.reshape(1, hidden)
    chan = jnp.transpose(chan_all, (1, 0, 2)).reshape(12, width)

    x = frames.reshape(count, length, width)
    dy = cotangent.reshape(count, length, width)
    calls = [(True, 2), (False, 3), (False, 2), (False, 1)]
    held = None
    base = 0
    pending = []
    starts = []
    for index, (grads, n) in enumerate(calls):
        early = index >= 2
        outs = run_block(
            grads, n, base, meta, x, dy, w_all, chan, bias, held,
            pending[index - 2] if early else (), starts[index - 2] if early else 0,
        )
        held = outs[:2]
        pending.append(tuple(swap(o, "tensor", t_n, 1) for o in outs[2:4]))
        starts.append(base)
        if grads:
            g_part, small_part, gbias_part = outs[4:]
        base += n
    held = place_received(starts[2], [2, 1], meta, held, pending[2] + pending[3])

    g = g_part.reshape(2, t_n // 2, 2, hidden_part, dp_n, width_part)
    g = fold(g, 2, "tensor", t_n, 1)
    g = fold(g.reshape(2, 2, 2, hidden_part, dp_n, width_part), 2, "tensor", t_n, 2)
    g = fold(g.reshape(2, 2, hidden_part, dp_n, width_part), 1, "tensor", t_n, 4)
    g = g.reshape(2, hidden_part, dp_n, width_part)
    bit = dp_n // 2
    while bit >= 1:
        g = fold(g, 2, "dp", dp_n, bit)
        bit //= 2
    g = g.reshape(2, hidden_part, width_part).astype(F32)
    shard_expand = g[0].T
    shard_project = g[1]

    small = jnp.concatenate([small_part.reshape(12 * width), gbias_part.reshape(hidden)])
    for bit in (1, 2, 4):
        small = small + swap(small, "tensor", t_n, bit)
    bit = 1
    while bit < dp_n:
        small = small + swap(small, "dp", dp_n, bit)
        bit *= 2
    g_small = lax.dynamic_slice_in_dim(small[: 12 * width].reshape(12, width), d * width_part, width_part, 1)
    g_bias = lax.dynamic_slice_in_dim(small[12 * width :], t * hidden_part, hidden_part, 0)
    back_sum = g_small[10]
    shard_channel = jnp.concatenate(
        [
            g_small[0:8],
            g_small[8:10] * 0.5,
            (back_sum * channel_param[11])[None],
            (g_small[11] * ROOT_HALF + back_sum * channel_param[10])[None],
        ],
        axis=0,
    )

    e_new, e_first, e_second = adam_update(expand_weight, expand_first, expand_second, shard_expand, 0.02)
    p_new, p_first, p_second = adam_update(project_weight, project_first, project_second, shard_project, 0.01)
    b_new, b_first, b_second = adam_update(hidden_bias, hidden_bias_first, hidden_bias_second, g_bias, 0.1)
    c_new, c_first, c_second = adam_update(channel_param, channel_first, channel_second, shard_channel, 0.2)
    return (
        held[0].reshape(frames.shape),
        held[1].reshape(frames.shape),
        e_new,
        e_first,
        e_second,
        e_new.astype(BF),
        p_new,
        p_first,
        p_second,
        p_new.astype(BF),
        b_new,
        b_first,
        b_second,
        c_new,
        c_first,
        c_second,
    )


def solution(mesh):
    frame_spec = P(None, "dp", None, None)
    e_spec = P("dp", "tensor")
    p_spec = P("tensor", "dp")
    b_spec = P("tensor")
    c_spec = P(None, "dp")
    in_specs = (
        (frame_spec, frame_spec, P(None, "dp")) + (e_spec,) * 3 + (p_spec,) * 3 + (b_spec,) * 3 + (c_spec,) * 3
    )
    out_specs = (frame_spec, frame_spec) + (e_spec,) * 4 + (p_spec,) * 4 + (b_spec,) * 3 + (c_spec,) * 3
    body = functools.partial(per_device, dp_n=mesh.shape["dp"], t_n=mesh.shape["tensor"])
    return jax.shard_map(body, mesh=mesh, in_specs=in_specs, out_specs=out_specs, check_vma=False)
```

```python
import functools
import math

import jax
import jax.numpy as jnp
import numpy as np
from jax import lax
from jax.experimental import pallas as pl
from jax.experimental.pallas import tpu as pltpu
from jax.sharding import PartitionSpec as P

MESH = pl.DeviceIdType.MESH
BF = jnp.bfloat16
F32 = jnp.float32
MIB = 1 << 20

eps_norm = 1e-06
beta_first = 0.5
beta_second = 0.5
adam_eps = 1e-08
decay_rate = 0.01
step_count = 6

ROOT_HALF = math.sqrt(0.5)
LOG2E = math.log2(math.e)
SLOPE_LOG = math.log2(2.0 / math.sqrt(math.pi))

BLOCK = 256
SUB = 16
LANES = 128
HCHUNK = 256
TILE = 16


def adam_update(weight, first, second, grad, rate):
    first_new = beta_first * first + (1.0 - beta_first) * grad
    second_new = beta_second * second + (1.0 - beta_second) * grad * grad
    first_hat = first_new / (1.0 - beta_first**step_count)
    second_hat = second_new / (1.0 - beta_second**step_count)
    weight_new = weight - rate * (
        first_hat / (jnp.sqrt(second_hat) + adam_eps) + decay_rate * weight
    )
    return (weight_new, first_new, second_new)


def gather_kernel(dp_n, t_n, w_ref, b_ref, c_ref, wg_ref, bg_ref, cg_ref, local_sem, ws, wr, bs, br, cs, cr):
    d = lax.axis_index("dp")
    t = lax.axis_index("tensor")
    rows = w_ref.shape[1]

    def piece(dd, tt):
        return wg_ref.at[dd, :, pl.ds(pl.multiple_of(tt * rows, 16), rows), :]

    barrier = pltpu.get_barrier_semaphore()
    for k in range(1, dp_n):
        pl.semaphore_signal(barrier, inc=1, device_id=(lax.rem(d + k, dp_n), t), device_id_type=MESH)
    for k in range(1, t_n):
        pl.semaphore_signal(barrier, inc=1, device_id=(d, jnp.bitwise_xor(t, k)), device_id_type=MESH)
    own_w = pltpu.make_async_copy(w_ref, piece(d, t), local_sem.at[0])
    own_b = pltpu.make_async_copy(b_ref, bg_ref.at[t], local_sem.at[1])
    own_c = pltpu.make_async_copy(c_ref, cg_ref.at[d], local_sem.at[2])
    own_w.start()
    own_b.start()
    own_c.start()
    pl.semaphore_wait(barrier, dp_n - 1 + t_n - 1)

    copies = []

    def send(src, dst, ssem, rsem, peer):
        copy = pltpu.make_async_remote_copy(
            src_ref=src, dst_ref=dst, send_sem=ssem, recv_sem=rsem, device_id=peer, device_id_type=MESH
        )
        copy.start()
        copies.append(copy)

    def arrived(dst, rsem):
        pltpu.make_async_copy(dst, dst, rsem).wait()

    for k in range(1, dp_n):
        peer = (lax.rem(d + k, dp_n), t)
        send(w_ref, piece(d, t), ws.at[0, k], wr.at[d, t], peer)
        send(c_ref, cg_ref.at[d], cs.at[k], cr.at[d], peer)
    for k in range(1, t_n):
        send(b_ref, bg_ref.at[t], bs.at[k], br.at[t], (d, jnp.bitwise_xor(t, k)))
    own_w.wait()
    own_b.wait()
    own_c.wait()
    sib = (d, jnp.bitwise_xor(t, 1))
    near = [jnp.bitwise_xor(t, 2), jnp.bitwise_xor(t, 4)]
    far = jnp.bitwise_xor(t, 6)
    order = [lax.rem(d + k, dp_n) for k in range(dp_n)]
    for k in range(dp_n):
        dd = order[k]
        if k > 0:
            arrived(piece(dd, t), wr.at[dd, t])
        for side in range(2):
            send(piece(dd, t), piece(dd, t), ws.at[1 + side, k], wr.at[dd, t], (d, near[side]))
        send(piece(dd, t), piece(dd, t), ws.at[3, k], wr.at[dd, t], sib)
    half = dp_n // 2
    for k in range(dp_n):
        dd = order[k]
        for side in range(2):
            arrived(piece(dd, near[side]), wr.at[dd, near[side]])
            if (k < half) == (side == 0):
                send(
                    piece(dd, near[side]),
                    piece(dd, near[side]),
                    ws.at[6, k],
                    wr.at[dd, near[side]],
                    (d, near[1 - side]),
                )
            send(piece(dd, near[side]), piece(dd, near[side]), ws.at[4 + side, k], wr.at[dd, near[side]], sib)
    for k in range(dp_n):
        dd = order[k]
        arrived(piece(dd, far), wr.at[dd, far])
        send(piece(dd, far), piece(dd, far), ws.at[7, k], wr.at[dd, far], sib)
    for k in range(dp_n):
        dd = order[k]
        for x in (1, 3, 5, 7):
            tt = jnp.bitwise_xor(t, x)
            arrived(piece(dd, tt), wr.at[dd, tt])
    for k in range(1, dp_n):
        dd = lax.rem(d + k, dp_n)
        arrived(cg_ref.at[dd], cr.at[dd])
    for k in range(1, t_n):
        tt = jnp.bitwise_xor(t, k)
        arrived(bg_ref.at[tt], br.at[tt])
    for copy in copies:
        copy.wait_send()


def gather_weights(dp_n, t_n, w_own, bias, channel):
    two, rows, width = w_own.shape
    return pl.pallas_call(
        functools.partial(gather_kernel, dp_n, t_n),
        out_shape=(
            jax.ShapeDtypeStruct((dp_n, two, rows * t_n, width), w_own.dtype),
            jax.ShapeDtypeStruct((t_n,) + bias.shape, bias.dtype),
            jax.ShapeDtypeStruct((dp_n,) + channel.shape, channel.dtype),
        ),
        in_specs=[pl.BlockSpec(memory_space=pl.ANY)] * 3,
        out_specs=(pl.BlockSpec(memory_space=pl.ANY),) * 3,
        scratch_shapes=[
            pltpu.SemaphoreType.DMA((3,)),
            pltpu.SemaphoreType.DMA((8, dp_n)),
            pltpu.SemaphoreType.DMA((dp_n, t_n)),
            pltpu.SemaphoreType.DMA((t_n,)),
            pltpu.SemaphoreType.DMA((t_n,)),
            pltpu.SemaphoreType.DMA((dp_n,)),
            pltpu.SemaphoreType.DMA((dp_n,)),
        ],
        compiler_params=pltpu.CompilerParams(collective_id=0, has_side_effects=True),
        name="gather_weights",
    )(w_own, bias, channel)


def dot_nn(a, b):
    return lax.dot_general(a, b, (((1,), (0,)), ((), ())), preferred_element_type=F32)


def dot_nt(a, b):
    return lax.dot_general(a, b, (((1,), (1,)), ((), ())), preferred_element_type=F32)


def split_rows(count, largest):
    step = largest
    while step >= TILE:
        yield step, count - lax.rem(count, 2 * step), lax.rem(lax.div(count, step), 2) == 1
        step //= 2


def block_kernel(grads, first, n, base, n_recv, rec_base, parts, length, width, hidden, *refs):
    refs = list(refs)
    meta, x_hbm, dy_hbm, w_hbm, chan, bias = refs[:6]
    refs = refs[6:]
    if not first:
        refs = refs[2:]
    received = refs[:n_recv]
    refs = refs[n_recv:]
    o_hbm = refs[:2]
    own_hbm = refs[2:4]
    token = refs[4]
    refs = refs[5:]
    if grads:
        g_out, small_out, gbias_out = refs[:3]
        refs = refs[3:]
    (x_pack, dy_pack, ob_pack, gb_pack, w_e, w_p) = refs[:6]
    xs, nh, rs, ds, nrm, dzs, br, dn2, hid, dpre, pre_s, dh_s, pc, pb, zero = refs[6:21]
    in_sem, out_sem, w_sem = refs[21:24]
    refs = refs[24:]
    if n_recv:
        stage, recv_sem = refs[:2]
        refs = refs[2:]
    if grads:
        gacc, left_t, gb_acc, sm_acc = refs
    groups = width // LANES
    R = BLOCK

    clip_of = [meta[base + k] for k in range(n)]
    len_of = [meta[8 + base + k] for k in range(n)]
    off = [jnp.int32(0)]
    for k in range(n):
        off.append(off[k] + lax.div(len_of[k] + 3 + TILE - 1, TILE) * TILE)
    tiles_of = [lax.div(len_of[k] + TILE - 1, TILE) * TILE for k in range(n)]
    nblk = lax.div(off[n] + TILE + R - 1, R)
    x_lead, dy_lead, ob_lead, gb_lead = TILE, R + TILE, R, R + TILE

    def aligned(v):
        return pl.multiple_of(v, TILE)

    w_copies = []
    for g in range(groups):
        w_copies.append(pltpu.make_async_copy(w_hbm.at[g, 0], w_e.at[:, pl.ds(g * LANES, LANES)], w_sem.at[0, g]))
        w_copies.append(pltpu.make_async_copy(w_hbm.at[g, 1], w_p.at[:, pl.ds(g * LANES, LANES)], w_sem.at[1, g]))

    def clip_in(k, act):
        for j, (src, dst, lead) in enumerate(((x_hbm, x_pack, x_lead), (dy_hbm, dy_pack, dy_lead))):
            for p, (size, start, have) in enumerate(split_rows(tiles_of[k], length)):

                @pl.when(have)
                def _():
                    copy = pltpu.make_async_copy(
                        src.at[clip_of[k], pl.ds(aligned(start), size), :],
                        dst.at[pl.ds(aligned(off[k] + lead + start), size), :],
                        in_sem.at[k, j, p],
                    )
                    act(copy)

    def clip_out(k, act):
        for j, (src, lead) in enumerate(((ob_pack, ob_lead), (gb_pack, gb_lead))):
            for which, dst in enumerate((o_hbm[j], own_hbm[j])):
                view = dst.at[clip_of[k]] if which == 0 else dst.at[k]
                p = 0
                for size, start, have in split_rows(tiles_of[k], length):

                    @pl.when(have)
                    def _():
                        copy = pltpu.make_async_copy(
                            src.at[pl.ds(aligned(off[k] + lead + start), size), :],
                            view.at[pl.ds(aligned(start), size), :],
                            out_sem.at[k, 2 * j + which, p],
                        )
                        act(copy)

                    p += 1
                rest = length - tiles_of[k]
                for size, start, have in split_rows(rest, length // 2):

                    @pl.when(have)
                    def _():
                        copy = pltpu.make_async_copy(
                            zero.at[pl.ds(0, size), :],
                            view.at[pl.ds(aligned(tiles_of[k] + start), size), :],
                            out_sem.at[k, 2 * j + which, p],
                        )
                        act(copy)

                    p += 1

    row_id = lax.broadcasted_iota(jnp.int32, (TILE, width), 0)

    def clear_tail(ref, k, lead):
        left = lax.rem(len_of[k], TILE)
        at = aligned(off[k] + len_of[k] - left + lead)

        @pl.when(left > 0)
        def _():
            tile = ref[pl.ds(at, TILE), :].astype(F32)
            ref[pl.ds(at, TILE), :] = jnp.where(row_id < left, tile, 0.0).astype(ref.dtype)

    def clear_gap(ref, k, lead):
        clear_tail(ref, k, lead)
        at = aligned(off[k] + tiles_of[k] + lead)

        @pl.when(off[k + 1] > off[k] + tiles_of[k])
        def _():
            ref[pl.ds(at, TILE), :] = jnp.zeros((TILE, width), ref.dtype)

    def clip_ready(k):
        clip_in(k, lambda c: c.wait())
        clear_gap(x_pack, k, x_lead)
        clear_gap(dy_pack, k, dy_lead)

    def clip_done(k):
        clear_tail(ob_pack, k, ob_lead)
        clear_tail(gb_pack, k, gb_lead)
        clip_out(k, lambda c: c.start())

    for k in range(n):
        clip_in(k, lambda c: c.start())
        if k == 0:
            for copy in w_copies:
                copy.start()
    recv_in, recv_out = [], []
    if n_recv:
        rec_n = received[0].shape[0]
        for j in range(2):
            for k in range(rec_n):
                recv_in.append(pltpu.make_async_copy(received[j].at[k], stage.at[j, k], recv_sem.at[0, j, k]))
                recv_out.append(
                    pltpu.make_async_copy(stage.at[j, k], o_hbm[j].at[meta[16 + rec_base + k]], recv_sem.at[1, j, k])
                )
        for copy in recv_in:
            copy.start()

    token[...] = jnp.zeros_like(token)
    zero[...] = jnp.zeros_like(zero)
    x_pack[pl.ds(0, x_lead), :] = jnp.zeros((x_lead, width), BF)
    dy_pack[pl.ds(0, dy_lead), :] = jnp.zeros((dy_lead, width), BF)

    @pl.loop(0, (R + 4 * TILE) // TILE)
    def _(s):
        at = off[n] + s * TILE
        x_pack[pl.ds(aligned(at + x_lead), TILE), :] = jnp.zeros((TILE, width), BF)
        dy_pack[pl.ds(aligned(at + dy_lead), TILE), :] = jnp.zeros((TILE, width), BF)

    for ref in (xs, nh, rs, br, dn2, ds):
        ref[...] = jnp.zeros_like(ref)
    if grads:
        gacc[...] = jnp.zeros_like(gacc)
        gb_acc[...] = jnp.zeros_like(gb_acc)
        sm_acc[...] = jnp.zeros_like(sm_acc)
    scale = chan[11:12, :]
    pc[0:8, :] = chan[0:8, :]
    pc[8:10, :] = chan[8:10, :] * ROOT_HALF
    pc[10:11, :] = scale * chan[10:11, :]
    pc[11:12, :] = scale
    pc[12:13, :] = scale * ROOT_HALF
    pc[13:14, :] = chan[8:9, :] * 0.5
    pb[...] = bias[...] * ROOT_HALF

    inv_c = 1.0 / width

    def lane(g):
        return slice(g * LANES, (g + 1) * LANES)

    def row(r, g):
        return pc[r : r + 1, lane(g)]

    def conv_tasks(b, q):
        top = b * R

        def ingest(s):
            for g in range(groups):
                xs[q, g, pl.ds(s, SUB), :] = x_pack[pl.ds(aligned(top + s), SUB), lane(g)].astype(F32)

        def conv_norm(s):
            conv = []
            for g in range(groups):
                acc = xs[q, g, pl.ds(s + 13, SUB), :] * row(0, g) + row(7, g)
                for k in range(1, 7):
                    acc = acc + xs[q, g, pl.ds(s + 13 + k, SUB), :] * row(k, g)
                conv.append(acc)
            mean = jnp.sum(sum(conv), axis=-1, keepdims=True) * inv_c
            cent = [v - mean for v in conv]
            var = jnp.sum(sum([v * v for v in cent]), axis=-1, keepdims=True) * inv_c
            inv = lax.rsqrt(var + eps_norm)
            rs[q, pl.ds(s, SUB), :] = jnp.broadcast_to(inv, (SUB, LANES))
            for g in range(groups):
                nhat = cent[g] * inv
                nh[q, g, pl.ds(s, SUB), :] = nhat
                nrm[pl.ds(s, SUB), lane(g)] = (nhat * row(8, g) + row(9, g)).astype(BF)
                dyf = dy_pack[pl.ds(aligned(top + dy_lead + s), SUB), lane(g)].astype(F32)
                dzs[pl.ds(s, SUB), lane(g)] = (dyf * row(11, g)).astype(BF)

        tasks = []
        lead = 2 * TILE
        for s in range(0, lead, SUB):
            tasks.append(functools.partial(ingest, s))
        for s in range(0, R, SUB):
            tasks.append(functools.partial(ingest, s + lead))
            tasks.append(functools.partial(conv_norm, s))
        return tasks

    def post_tasks(b, q):
        top = b * R

        def norm_back(s):
            dn, prod = [], []
            for g in range(groups):
                bv = br[pl.ds(s, SUB), lane(g)]
                x_mid = xs[q, g, pl.ds(s + TILE, SUB), :]
                ob = (x_mid + row(10, g)) + bv * row(12, g)
                ob_pack[pl.ds(aligned(top + ob_lead + s), SUB), lane(g)] = ob.astype(BF)
                d2 = dn2[pl.ds(s, SUB), lane(g)]
                nhat = nh[q, g, pl.ds(s, SUB), :]
                dg = d2 * row(13, g)
                dn.append(dg)
                prod.append(dg * nhat)
                if grads:
                    p2 = d2 * nhat
                    dyf = dy_pack[pl.ds(aligned(top + dy_lead + s), SUB), lane(g)].astype(F32)
                    dyb = dyf * bv
                    sm_acc[g, 8] += p2[0:8] + p2[8:16]
                    sm_acc[g, 9] += d2[0:8] + d2[8:16]
                    sm_acc[g, 10] += dyf[0:8] + dyf[8:16]
                    sm_acc[g, 11] += dyb[0:8] + dyb[8:16]
            m1 = jnp.sum(sum(dn), axis=-1, keepdims=True) * inv_c
            m2 = jnp.sum(sum(prod), axis=-1, keepdims=True) * inv_c
            inv = rs[q, pl.ds(s, SUB), :]
            for g in range(groups):
                nhat = nh[q, g, pl.ds(s, SUB), :]
                dconv = inv * (dn[g] - m1 - nhat * m2)
                ds[g, pl.ds(2 * TILE + s, SUB), :] = dconv
                if grads:
                    sm_acc[g, 7] += dconv[0:8] + dconv[8:16]
                    for k in range(7):
                        tp = dconv * xs[q, g, pl.ds(s + 13 + k, SUB), :]
                        sm_acc[g, k] += tp[0:8] + tp[8:16]

        def carry():
            for g in range(groups):
                ds[g, pl.ds(0, 2 * TILE), :] = ds[g, pl.ds(R, 2 * TILE), :]

        return [carry] + [functools.partial(norm_back, s) for s in range(0, R, SUB)]

    def frame_tasks(b):
        top = b * R

        def frames_back(s):
            for g in range(groups):
                acc = dy_pack[pl.ds(aligned(top + R + s), SUB), lane(g)].astype(F32)
                for k in range(7):
                    acc = acc + ds[g, pl.ds(s + 19 - k, SUB), :] * row(k, g)
                gb_pack[pl.ds(aligned(top + R + s), SUB), lane(g)] = acc.astype(BF)

        return [functools.partial(frames_back, s) for s in range(0, R, SUB)]

    def up_step(c):
        cols = slice(c * HCHUNK, (c + 1) * HCHUNK)

        def one():
            pre_s[c % 2] = dot_nt(nrm[...], w_e[cols, :])

        def two():
            dh_s[c % 2] = dot_nt(dzs[...], w_p[cols, :])

        return [one, two]

    def gelu_tasks(c):
        cols = slice(c * HCHUNK, (c + 1) * HCHUNK)

        def part(s):
            u = pre_s[c % 2, pl.ds(s, SUB), :] + pb[0:1, cols]
            v = 1.0 + lax.erf(u)
            hid[pl.ds(s, SUB), cols] = (u * v).astype(BF)
            e = jnp.exp2(SLOPE_LOG - LOG2E * (u * u))
            dp2 = dh_s[c % 2, pl.ds(s, SUB), :] * (v + u * e)
            dpre[pl.ds(s, SUB), cols] = dp2.astype(BF)
            if grads:
                gb_acc[:, cols] += dp2[0:8] + dp2[8:16]

        return [functools.partial(part, s) for s in range(0, R, SUB)]

    def down_steps():
        steps = []
        for h in range(2):
            cols = slice(h * (width // 2), (h + 1) * (width // 2))

            def one(cols=cols):
                br[:, cols] = dot_nn(hid[...], w_p[:, cols])

            def two(cols=cols):
                dn2[:, cols] = dot_nn(dpre[...], w_e[:, cols])

            steps += [one, two]
        return steps

    def grad_steps():
        steps = []

        def turn():
            left_t[0] = nrm[...].T
            left_t[1] = dzs[...].T

        for c in range(hidden // HCHUNK):
            cols = slice(c * HCHUNK, (c + 1) * HCHUNK)
            for which, right in enumerate((dpre, hid)):

                def step(which=which, right=right, cols=cols):
                    gacc[which, :, cols] += dot_nn(left_t[which], right[:, cols])

                steps.append(step)
        return turn, steps

    def interleave(steps, tasks):
        done = 0
        for index, step in enumerate(steps):
            step()
            upto = len(tasks) * (index + 1) // len(steps)
            while done < upto:
                tasks[done]()
                done += 1

    def merge(first_list, second_list):
        total = [(index / len(part), which, task) for which, part in enumerate((first_list, second_list)) for index, task in enumerate(part)]
        return [task for _, _, task in sorted(total, key=lambda item: item[:2])]

    def run_tasks(tasks):
        for task in tasks:
            task()

    for k in range(n):

        @pl.when(off[k] < R + TILE)
        def _():
            clip_ready(k)

    run_tasks(conv_tasks(0, 0))
    for copy in w_copies:
        copy.wait()
    n_chunk = hidden // HCHUNK

    @pl.loop(0, nblk)
    def _(i):
        q = lax.rem(i, 2)
        for k in range(n):

            @pl.when((off[k] >= (i + 1) * R + TILE) & (off[k] < (i + 2) * R + TILE))
            def _():
                clip_ready(k)

        post = post_tasks(i - 1, 1 - q)
        for c in range(n_chunk):
            mine = post[len(post) * c // n_chunk : len(post) * (c + 1) // n_chunk]
            interleave(up_step(c), merge(gelu_tasks(c - 1), mine) if c else mine)
        run_tasks(gelu_tasks(n_chunk - 1))
        rest = merge(conv_tasks(i + 1, 1 - q), frame_tasks(i - 1))
        if grads:
            turn, steps = grad_steps()
            turn()
            interleave(down_steps() + steps, rest)
        else:
            interleave(down_steps(), rest)

        if n_recv:

            @pl.when(i == 0)
            def _():
                for copy in recv_in:
                    copy.wait()
                for copy in recv_out:
                    copy.start()

        for k in range(n):
            end = off[k] + len_of[k] + TILE

            @pl.when((end > (i - 1) * R) & (end <= i * R))
            def _():
                clip_done(k)

    run_tasks(post_tasks(nblk - 1, lax.rem(nblk - 1, 2)))
    run_tasks(frame_tasks(nblk - 1))
    for k in range(n):

        @pl.when(off[k] + len_of[k] + TILE > (nblk - 1) * R)
        def _():
            clip_done(k)

    if grads:
        share = hidden // parts
        piece = math.gcd(share, HCHUNK)
        for which in range(2):
            for c in range(hidden // HCHUNK):
                cols = slice(c * HCHUNK, (c + 1) * HCHUNK)
                turned = (gacc[which, :, cols] * ROOT_HALF).T.astype(BF)
                for h in range(0, HCHUNK, piece):
                    t_of, r_of = divmod(c * HCHUNK + h, share)
                    for g in range(groups):
                        g_out[t_of % 2, t_of // 2, g, which, pl.ds(r_of, piece), :] = turned[h : h + piece, lane(g)]
        gbias_out[...] = jnp.sum(gb_acc[...], axis=0, keepdims=True) * 0.5
        for g in range(groups):
            for k in range(12):
                small_out[k : k + 1, lane(g)] = jnp.sum(sm_acc[g, k], axis=0, keepdims=True)
    for k in range(n):
        clip_out(k, lambda c: c.wait())
    for copy in recv_out:
        copy.wait()


def run_block(grads, n, base, meta, x, dy, w, chan, bias, held, received, rec_base, parts):
    clips, length, width = x.shape
    hidden = w.shape[2]
    groups = width // LANES
    first = held is None
    R = BLOCK
    rows = n * (length + TILE) + 3 * R + 8 * TILE
    out_shape = [jax.ShapeDtypeStruct((clips, length, width), BF)] * 2 + [
        jax.ShapeDtypeStruct((n, length, width), BF)
    ] * 2
    any_spec = pl.BlockSpec(memory_space=pl.ANY)
    vmem_spec = pl.BlockSpec(memory_space=pltpu.VMEM)
    out_shape.append(jax.ShapeDtypeStruct((8, LANES), F32))
    out_specs = [any_spec] * 4 + [vmem_spec]
    if grads:
        out_shape += [
            jax.ShapeDtypeStruct((2, parts // 2, groups, 2, hidden // parts, LANES), BF),
            jax.ShapeDtypeStruct((12, width), F32),
            jax.ShapeDtypeStruct((1, hidden), F32),
        ]
        out_specs += [vmem_spec] * 3
    args = [meta, x, dy, w, chan, bias]
    in_specs = [
        pl.BlockSpec(memory_space=pltpu.SMEM),
        any_spec,
        any_spec,
        any_spec,
        vmem_spec,
        vmem_spec,
    ]
    aliases = {}
    if not first:
        aliases = {6: 0, 7: 1}
        args += list(held)
        in_specs += [any_spec] * 2
    args += list(received)
    in_specs += [any_spec] * len(received)
    scratch = [pltpu.VMEM((rows, width), BF)] * 4 + [pltpu.VMEM((hidden, width), BF)] * 2
    scratch += [
        pltpu.VMEM((2, groups, R + 2 * TILE, LANES), F32),
        pltpu.VMEM((2, groups, R, LANES), F32),
        pltpu.VMEM((2, R, LANES), F32),
        pltpu.VMEM((groups, R + 2 * TILE, LANES), F32),
    ]
    scratch += [pltpu.VMEM((R, width), BF)] * 2
    scratch += [pltpu.VMEM((R, width), F32)] * 2
    scratch += [pltpu.VMEM((R, hidden), BF)] * 2
    scratch += [pltpu.VMEM((2, R, HCHUNK), F32)] * 2
    scratch += [
        pltpu.VMEM((16, width), F32),
        pltpu.VMEM((1, hidden), F32),
        pltpu.VMEM((length // 2, width), BF),
        pltpu.SemaphoreType.DMA((n, 2, 8)),
        pltpu.SemaphoreType.DMA((n, 4, 16)),
        pltpu.SemaphoreType.DMA((2, groups)),
    ]
    if received:
        rec_n = received[0].shape[0]
        scratch += [pltpu.VMEM((2, rec_n, length, width), BF), pltpu.SemaphoreType.DMA((2, 2, rec_n))]
    if grads:
        scratch += [
            pltpu.VMEM((2, width, hidden), F32),
            pltpu.VMEM((2, width, R), BF),
            pltpu.VMEM((8, hidden), F32),
            pltpu.VMEM((groups, 12, 8, LANES), F32),
        ]
    per_row = 2 * width * hidden * (6 if grads else 4)
    cost = pl.CostEstimate(
        flops=int(per_row * n * length * 1.5), bytes_accessed=n * length * width * 12, transcendentals=0
    )
    return pl.pallas_call(
        functools.partial(block_kernel, grads, first, n, base, len(received), rec_base, parts, length, width, hidden),
        out_shape=tuple(out_shape),
        in_specs=in_specs,
        out_specs=tuple(out_specs),
        scratch_shapes=scratch,
        input_output_aliases=aliases,
        cost_estimate=cost,
        compiler_params=pltpu.CompilerParams(vmem_limit_bytes=56 * MIB),
        name="block_grads" if grads else "block_plain",
    )(*args)


def place_kernel(base, counts, meta, *refs):
    n_in = 2 + 2 * len(counts)
    ins = refs[2:n_in]
    outs = refs[n_in : n_in + 2]
    stage, sem = refs[n_in + 2 :]
    taken, placed = [], []
    at = 0
    for block, count in enumerate(counts):
        for k in range(count):
            for j in range(2):
                taken.append(pltpu.make_async_copy(ins[2 * block + j].at[k], stage.at[j, at], sem.at[0, j, at]))
                placed.append(
                    pltpu.make_async_copy(stage.at[j, at], outs[j].at[meta[16 + base + at]], sem.at[1, j, at])
                )
            at += 1
    for copy in taken:
        copy.start()
    for one, two in zip(taken, placed):
        one.wait()
        two.start()
    for copy in placed:
        copy.wait()


def place_received(base, counts, meta, held, arrays):
    any_spec = pl.BlockSpec(memory_space=pl.ANY)
    length, width = held[0].shape[1:]
    total = sum(counts)
    return pl.pallas_call(
        functools.partial(place_kernel, base, counts),
        out_shape=tuple(jax.ShapeDtypeStruct(h.shape, h.dtype) for h in held),
        in_specs=[pl.BlockSpec(memory_space=pltpu.SMEM)] + [any_spec] * (2 + len(arrays)),
        out_specs=(any_spec,) * 2,
        scratch_shapes=[pltpu.VMEM((2, total, length, width), BF), pltpu.SemaphoreType.DMA((2, 2, total))],
        input_output_aliases={1: 0, 2: 1},
        compiler_params=pltpu.CompilerParams(vmem_limit_bytes=40 * MIB),
        name="place_received",
    )(meta, *held, *arrays)


def swap(value, axis, size, bit):
    return lax.ppermute(value, axis, [(i, i ^ bit) for i in range(size)])


def after(value, token):
    return lax.optimization_barrier((value, token))[0]


def tree_sum(values):
    while len(values) > 1:
        values = [values[i] + values[i + 1] for i in range(0, len(values), 2)]
    return values[0]


def pick(value, index):
    return lax.dynamic_index_in_dim(value, index, 0, keepdims=False)


def spread(value, axis, size, me, step, token):
    got = [swap(pick(value, me ^ k), axis, size, k * step) for k in range(1, value.shape[0])]
    got = [after(v, token) for v in got]
    return tree_sum([pick(value, me).astype(F32)] + [v.astype(F32) for v in got])


def total_over(value, axis, size, step, count, token):
    got = [after(swap(value, axis, size, k * step), token) for k in range(1, count)]
    return tree_sum([value] + got)


def per_device(
    frames,
    cotangent,
    lengths,
    expand_weight,
    expand_first,
    expand_second,
    project_weight,
    project_first,
    project_second,
    hidden_bias,
    hidden_bias_first,
    hidden_bias_second,
    channel_param,
    channel_first,
    channel_second,
    *,
    dp_n,
    t_n,
):
    micro, clips, length, width = frames.shape
    hidden_part = expand_weight.shape[1]
    hidden = hidden_part * t_n
    width_part = expand_weight.shape[0]
    count = micro * clips
    d = lax.axis_index("dp")
    t = lax.axis_index("tensor")

    lens = lengths.reshape(count)
    ids = jnp.arange(count, dtype=jnp.int32)
    ahead = (lens[None, :] > lens[:, None]) | ((lens[None, :] == lens[:, None]) & (ids[None, :] < ids[:, None]))
    rank = jnp.sum(ahead.astype(jnp.int32), axis=1)
    per_core = count // 2
    table = np.zeros((t_n, per_core), np.int32)
    for tt in range(t_n):
        core, chip = tt % 2, tt // 2
        own = [4 * (j // 2) + (3 * (j % 2) if core == 0 else 1 + (j % 2)) for j in range(per_core)]
        pair = [chip, per_core - 1 - chip]
        table[tt] = [own[j] for j in pair] + [own[j] for j in range(per_core) if j not in pair]
    both = np.concatenate([table, table[np.arange(t_n) ^ 1]], axis=1)
    wanted = lax.dynamic_slice_in_dim(jnp.asarray(both), t, 1, 0).reshape(2 * per_core)
    hit = (rank[None, :] == wanted[:, None]).astype(jnp.int32)
    seq = jnp.sum(hit * ids[None, :], axis=1)
    seq_len = jnp.sum(hit * lens[None, :], axis=1)
    meta = jnp.concatenate([seq[:per_core], seq_len[:per_core], seq[per_core:]])

    w_own = jnp.stack([expand_weight.T.astype(BF), project_weight.astype(BF)])
    w_all, bias_all, chan_all = gather_weights(dp_n, t_n, w_own, hidden_bias.reshape(1, hidden_part), channel_param)
    if width_part != LANES:
        w_all = jnp.transpose(w_all, (1, 2, 0, 3)).reshape(2, hidden, width // LANES, LANES)
        w_all = jnp.transpose(w_all, (2, 0, 1, 3))
    bias = bias_all.reshape(1, hidden)
    chan = jnp.transpose(chan_all, (1, 0, 2)).reshape(12, width)

    x = frames.reshape(count, length, width)
    dy = cotangent.reshape(count, length, width)
    calls = [(True, 2), (False, 3), (False, 2), (False, 1)]
    held = None
    base = 0
    pending = []
    starts = []
    tokens = []
    for index, (grads, n) in enumerate(calls):
        early = index >= 2
        outs = run_block(
            grads, n, base, meta, x, dy, w_all, chan, bias, held,
            pending[index - 2] if early else (), starts[index - 2] if early else 0, t_n,
        )
        held = outs[:2]
        pending.append(tuple(swap(o, "tensor", t_n, 1) for o in outs[2:4]))
        starts.append(base)
        tokens.append(outs[4])
        if grads:
            g_part, small_part, gbias_part = outs[5:]
        base += n
    held = place_received(starts[2], [2, 1], meta, held, pending[2] + pending[3])

    if width_part != LANES:
        g_part = g_part.reshape(g_part.shape[:-1] + (LANES // width_part, width_part))
        g_part = jnp.transpose(g_part, (0, 1, 2, 5, 3, 4, 6))
        g_part = g_part.reshape(2, t_n // 2, dp_n, 2, hidden_part, width_part)
    core, chip = lax.rem(t, 2), lax.div(t, 2)
    g = spread(g_part, "tensor", t_n, core, 1, tokens[1]).astype(BF)
    g = spread(g, "tensor", t_n, chip, 2, tokens[2]).astype(BF)
    g = spread(g, "dp", dp_n, d, 1, tokens[3])
    shard_expand = g[0].T
    shard_project = g[1]

    small = jnp.concatenate([small_part.reshape(12 * width), gbias_part.reshape(hidden)])
    small = total_over(small, "tensor", t_n, 1, 2, tokens[1])
    small = total_over(small, "tensor", t_n, 2, t_n // 2, tokens[2])
    small = total_over(small, "dp", dp_n, 1, dp_n, tokens[3])
    g_small = lax.dynamic_slice_in_dim(small[: 12 * width].reshape(12, width), d * width_part, width_part, 1)
    g_bias = lax.dynamic_slice_in_dim(small[12 * width :], t * hidden_part, hidden_part, 0)
    back_sum = g_small[10]
    shard_channel = jnp.concatenate(
        [
            g_small[0:8],
            g_small[8:10] * 0.5,
            (back_sum * channel_param[11])[None],
            (g_small[11] * ROOT_HALF + back_sum * channel_param[10])[None],
        ],
        axis=0,
    )

    e_new, e_first, e_second = adam_update(expand_weight, expand_first, expand_second, shard_expand, 0.02)
    p_new, p_first, p_second = adam_update(project_weight, project_first, project_second, shard_project, 0.01)
    b_new, b_first, b_second = adam_update(hidden_bias, hidden_bias_first, hidden_bias_second, g_bias, 0.1)
    c_new, c_first, c_second = adam_update(channel_param, channel_first, channel_second, shard_channel, 0.2)
    return (
        held[0].reshape(frames.shape),
        held[1].reshape(frames.shape),
        e_new,
        e_first,
        e_second,
        e_new.astype(BF),
        p_new,
        p_first,
        p_second,
        p_new.astype(BF),
        b_new,
        b_first,
        b_second,
        c_new,
        c_first,
        c_second,
    )


def solution(mesh):
    frame_spec = P(None, "dp", None, None)
    e_spec = P("dp", "tensor")
    p_spec = P("tensor", "dp")
    b_spec = P("tensor")
    c_spec = P(None, "dp")
    in_specs = (
        (frame_spec, frame_spec, P(None, "dp")) + (e_spec,) * 3 + (p_spec,) * 3 + (b_spec,) * 3 + (c_spec,) * 3
    )
    out_specs = (frame_spec, frame_spec) + (e_spec,) * 4 + (p_spec,) * 4 + (b_spec,) * 3 + (c_spec,) * 3
    body = functools.partial(per_device, dp_n=mesh.shape["dp"], t_n=mesh.shape["tensor"])
    return jax.shard_map(body, mesh=mesh, in_specs=in_specs, out_specs=out_specs, check_vma=False)
```

```python
import functools
import math

import jax
import jax.numpy as jnp
import numpy as np
from jax import lax
from jax.experimental import pallas as pl
from jax.experimental.pallas import tpu as pltpu
from jax.sharding import PartitionSpec as P

MESH = pl.DeviceIdType.MESH
BF = jnp.bfloat16
F32 = jnp.float32
MIB = 1 << 20

eps_norm = 1e-06
beta_first = 0.5
beta_second = 0.5
adam_eps = 1e-08
decay_rate = 0.01
step_count = 6

ROOT_HALF = math.sqrt(0.5)
LOG2E = math.log2(math.e)
SLOPE_LOG = math.log2(2.0 / math.sqrt(math.pi))

BLOCK = 256
SUB = 16
LANES = 128
HCHUNK = 256
TILE = 16


def adam_update(weight, first, second, grad, rate):
    first_new = beta_first * first + (1.0 - beta_first) * grad
    second_new = beta_second * second + (1.0 - beta_second) * grad * grad
    first_hat = first_new / (1.0 - beta_first**step_count)
    second_hat = second_new / (1.0 - beta_second**step_count)
    weight_new = weight - rate * (
        first_hat / (jnp.sqrt(second_hat) + adam_eps) + decay_rate * weight
    )
    return (weight_new, first_new, second_new)


def gather_kernel(dp_n, t_n, w_ref, b_ref, c_ref, wg_ref, bg_ref, cg_ref, local_sem, ws, wr, bs, br, cs, cr):
    d = lax.axis_index("dp")
    t = lax.axis_index("tensor")
    rows = w_ref.shape[1]

    def piece(dd, tt):
        return wg_ref.at[dd, :, pl.ds(pl.multiple_of(tt * rows, 16), rows), :]

    barrier = pltpu.get_barrier_semaphore()
    for k in range(1, dp_n):
        pl.semaphore_signal(barrier, inc=1, device_id=(lax.rem(d + k, dp_n), t), device_id_type=MESH)
    for k in range(1, t_n):
        pl.semaphore_signal(barrier, inc=1, device_id=(d, jnp.bitwise_xor(t, k)), device_id_type=MESH)
    own_w = pltpu.make_async_copy(w_ref, piece(d, t), local_sem.at[0])
    own_b = pltpu.make_async_copy(b_ref, bg_ref.at[t], local_sem.at[1])
    own_c = pltpu.make_async_copy(c_ref, cg_ref.at[d], local_sem.at[2])
    own_w.start()
    own_b.start()
    own_c.start()
    pl.semaphore_wait(barrier, dp_n - 1 + t_n - 1)

    copies = []

    def send(src, dst, ssem, rsem, peer):
        copy = pltpu.make_async_remote_copy(
            src_ref=src, dst_ref=dst, send_sem=ssem, recv_sem=rsem, device_id=peer, device_id_type=MESH
        )
        copy.start()
        copies.append(copy)

    def arrived(dst, rsem):
        pltpu.make_async_copy(dst, dst, rsem).wait()

    for k in range(1, dp_n):
        peer = (lax.rem(d + k, dp_n), t)
        send(w_ref, piece(d, t), ws.at[0, k], wr.at[d, t], peer)
        send(c_ref, cg_ref.at[d], cs.at[k], cr.at[d], peer)
    for k in range(1, t_n):
        send(b_ref, bg_ref.at[t], bs.at[k], br.at[t], (d, jnp.bitwise_xor(t, k)))
    own_w.wait()
    own_b.wait()
    own_c.wait()
    sib = (d, jnp.bitwise_xor(t, 1))
    near = [jnp.bitwise_xor(t, 2), jnp.bitwise_xor(t, 4)]
    far = jnp.bitwise_xor(t, 6)
    order = [lax.rem(d + k, dp_n) for k in range(dp_n)]
    for k in range(dp_n):
        dd = order[k]
        if k > 0:
            arrived(piece(dd, t), wr.at[dd, t])
        for side in range(2):
            send(piece(dd, t), piece(dd, t), ws.at[1 + side, k], wr.at[dd, t], (d, near[side]))
        send(piece(dd, t), piece(dd, t), ws.at[3, k], wr.at[dd, t], sib)
    half = dp_n // 2
    for k in range(dp_n):
        dd = order[k]
        for side in range(2):
            arrived(piece(dd, near[side]), wr.at[dd, near[side]])
            if (k < half) == (side == 0):
                send(
                    piece(dd, near[side]),
                    piece(dd, near[side]),
                    ws.at[6, k],
                    wr.at[dd, near[side]],
                    (d, near[1 - side]),
                )
            send(piece(dd, near[side]), piece(dd, near[side]), ws.at[4 + side, k], wr.at[dd, near[side]], sib)
    for k in range(dp_n):
        dd = order[k]
        arrived(piece(dd, far), wr.at[dd, far])
        send(piece(dd, far), piece(dd, far), ws.at[7, k], wr.at[dd, far], sib)
    for k in range(dp_n):
        dd = order[k]
        for x in (1, 3, 5, 7):
            tt = jnp.bitwise_xor(t, x)
            arrived(piece(dd, tt), wr.at[dd, tt])
    for k in range(1, dp_n):
        dd = lax.rem(d + k, dp_n)
        arrived(cg_ref.at[dd], cr.at[dd])
    for k in range(1, t_n):
        tt = jnp.bitwise_xor(t, k)
        arrived(bg_ref.at[tt], br.at[tt])
    for copy in copies:
        copy.wait_send()


def gather_weights(dp_n, t_n, w_own, bias, channel):
    two, rows, width = w_own.shape
    return pl.pallas_call(
        functools.partial(gather_kernel, dp_n, t_n),
        out_shape=(
            jax.ShapeDtypeStruct((dp_n, two, rows * t_n, width), w_own.dtype),
            jax.ShapeDtypeStruct((t_n,) + bias.shape, bias.dtype),
            jax.ShapeDtypeStruct((dp_n,) + channel.shape, channel.dtype),
        ),
        in_specs=[pl.BlockSpec(memory_space=pl.ANY)] * 3,
        out_specs=(pl.BlockSpec(memory_space=pl.ANY),) * 3,
        scratch_shapes=[
            pltpu.SemaphoreType.DMA((3,)),
            pltpu.SemaphoreType.DMA((8, dp_n)),
            pltpu.SemaphoreType.DMA((dp_n, t_n)),
            pltpu.SemaphoreType.DMA((t_n,)),
            pltpu.SemaphoreType.DMA((t_n,)),
            pltpu.SemaphoreType.DMA((dp_n,)),
            pltpu.SemaphoreType.DMA((dp_n,)),
        ],
        compiler_params=pltpu.CompilerParams(collective_id=0, has_side_effects=True),
        name="gather_weights",
    )(w_own, bias, channel)


def dot_nn(a, b):
    return lax.dot_general(a, b, (((1,), (0,)), ((), ())), preferred_element_type=F32)


def dot_nt(a, b):
    return lax.dot_general(a, b, (((1,), (1,)), ((), ())), preferred_element_type=F32)


def split_rows(count, largest):
    step = largest
    while step >= TILE:
        yield step, count - lax.rem(count, 2 * step), lax.rem(lax.div(count, step), 2) == 1
        step //= 2


def block_kernel(grads, first, n, base, n_recv, rec_base, parts, length, width, hidden, *refs):
    refs = list(refs)
    meta, x_hbm, dy_hbm, w_hbm, chan, bias = refs[:6]
    refs = refs[6:]
    if not first:
        refs = refs[2:]
    received = refs[:n_recv]
    refs = refs[n_recv:]
    o_hbm = refs[:2]
    own_hbm = refs[2:4]
    token = refs[4]
    refs = refs[5:]
    if grads:
        g_out, small_out, gbias_out = refs[:3]
        refs = refs[3:]
    (x_pack, dy_pack, ob_pack, gb_pack, w_e, w_p) = refs[:6]
    xs, nh, rs, ds, nrm, dzs, br, dn2, hid, dpre, pre_s, dh_s, pc, pb, zero = refs[6:21]
    in_sem, out_sem, w_sem = refs[21:24]
    refs = refs[24:]
    if n_recv:
        stage, recv_sem = refs[:2]
        refs = refs[2:]
    if grads:
        gacc, left_t, gb_acc, sm_acc = refs
    groups = width // LANES
    R = BLOCK

    clip_of = [meta[base + k] for k in range(n)]
    len_of = [meta[8 + base + k] for k in range(n)]
    off = [jnp.int32(0)]
    for k in range(n):
        off.append(off[k] + lax.div(len_of[k] + 3 + TILE - 1, TILE) * TILE)
    tiles_of = [lax.div(len_of[k] + TILE - 1, TILE) * TILE for k in range(n)]
    nblk = lax.div(off[n] + TILE + R - 1, R)
    x_lead, dy_lead, ob_lead, gb_lead = TILE, R + TILE, R, R + TILE

    def aligned(v):
        return pl.multiple_of(v, TILE)

    w_copies = []
    for g in range(groups):
        w_copies.append(pltpu.make_async_copy(w_hbm.at[g, 0], w_e.at[:, pl.ds(g * LANES, LANES)], w_sem.at[0, g]))
        w_copies.append(pltpu.make_async_copy(w_hbm.at[g, 1], w_p.at[:, pl.ds(g * LANES, LANES)], w_sem.at[1, g]))

    def clip_in(k, act):
        for j, (src, dst, lead) in enumerate(((x_hbm, x_pack, x_lead), (dy_hbm, dy_pack, dy_lead))):
            for p, (size, start, have) in enumerate(split_rows(tiles_of[k], length)):

                @pl.when(have)
                def _():
                    copy = pltpu.make_async_copy(
                        src.at[clip_of[k], pl.ds(aligned(start), size), :],
                        dst.at[pl.ds(aligned(off[k] + lead + start), size), :],
                        in_sem.at[k, j, p],
                    )
                    act(copy)

    def clip_out(k, act):
        for j, (src, lead) in enumerate(((ob_pack, ob_lead), (gb_pack, gb_lead))):
            for which, dst in enumerate((o_hbm[j], own_hbm[j])):
                view = dst.at[clip_of[k]] if which == 0 else dst.at[k]
                p = 0
                for size, start, have in split_rows(tiles_of[k], length):

                    @pl.when(have)
                    def _():
                        copy = pltpu.make_async_copy(
                            src.at[pl.ds(aligned(off[k] + lead + start), size), :],
                            view.at[pl.ds(aligned(start), size), :],
                            out_sem.at[k, 2 * j + which, p],
                        )
                        act(copy)

                    p += 1
                rest = length - tiles_of[k]
                for size, start, have in split_rows(rest, length // 2):

                    @pl.when(have)
                    def _():
                        copy = pltpu.make_async_copy(
                            zero.at[pl.ds(0, size), :],
                            view.at[pl.ds(aligned(tiles_of[k] + start), size), :],
                            out_sem.at[k, 2 * j + which, p],
                        )
                        act(copy)

                    p += 1

    row_id = lax.broadcasted_iota(jnp.int32, (TILE, width), 0)

    def clear_tail(ref, k, lead):
        left = lax.rem(len_of[k], TILE)
        at = aligned(off[k] + len_of[k] - left + lead)

        @pl.when(left > 0)
        def _():
            tile = ref[pl.ds(at, TILE), :].astype(F32)
            ref[pl.ds(at, TILE), :] = jnp.where(row_id < left, tile, 0.0).astype(ref.dtype)

    def clear_gap(ref, k, lead):
        clear_tail(ref, k, lead)
        at = aligned(off[k] + tiles_of[k] + lead)

        @pl.when(off[k + 1] > off[k] + tiles_of[k])
        def _():
            ref[pl.ds(at, TILE), :] = jnp.zeros((TILE, width), ref.dtype)

    def clip_ready(k):
        clip_in(k, lambda c: c.wait())
        clear_gap(x_pack, k, x_lead)
        clear_gap(dy_pack, k, dy_lead)

    def clip_done(k):
        clear_tail(ob_pack, k, ob_lead)
        clear_tail(gb_pack, k, gb_lead)
        clip_out(k, lambda c: c.start())

    for k in range(n):
        clip_in(k, lambda c: c.start())
        if k == 0:
            for copy in w_copies:
                copy.start()
    recv_in, recv_out = [], []
    if n_recv:
        rec_n = received[0].shape[0]
        for j in range(2):
            for k in range(rec_n):
                recv_in.append(pltpu.make_async_copy(received[j].at[k], stage.at[j, k], recv_sem.at[0, j, k]))
                recv_out.append(
                    pltpu.make_async_copy(stage.at[j, k], o_hbm[j].at[meta[16 + rec_base + k]], recv_sem.at[1, j, k])
                )
        for copy in recv_in:
            copy.start()

    token[...] = jnp.zeros_like(token)
    zero[...] = jnp.zeros_like(zero)
    x_pack[pl.ds(0, x_lead), :] = jnp.zeros((x_lead, width), BF)
    dy_pack[pl.ds(0, dy_lead), :] = jnp.zeros((dy_lead, width), BF)

    @pl.loop(0, (R + 4 * TILE) // TILE)
    def _(s):
        at = off[n] + s * TILE
        x_pack[pl.ds(aligned(at + x_lead), TILE), :] = jnp.zeros((TILE, width), BF)
        dy_pack[pl.ds(aligned(at + dy_lead), TILE), :] = jnp.zeros((TILE, width), BF)

    for ref in (xs, nh, rs, br, dn2, ds):
        ref[...] = jnp.zeros_like(ref)
    if grads:
        gacc[...] = jnp.zeros_like(gacc)
        gb_acc[...] = jnp.zeros_like(gb_acc)
        sm_acc[...] = jnp.zeros_like(sm_acc)
    scale = chan[11:12, :]
    pc[0:8, :] = chan[0:8, :]
    pc[8:10, :] = chan[8:10, :] * ROOT_HALF
    pc[10:11, :] = scale * chan[10:11, :]
    pc[11:12, :] = scale
    pc[12:13, :] = scale * ROOT_HALF
    pc[13:14, :] = chan[8:9, :] * 0.5
    pb[...] = bias[...] * ROOT_HALF

    inv_c = 1.0 / width

    def lane(g):
        return slice(g * LANES, (g + 1) * LANES)

    def row(r, g):
        return pc[r : r + 1, lane(g)]

    def conv_tasks(b, q):
        top = b * R

        def ingest(s):
            for g in range(groups):
                xs[q, g, pl.ds(s, SUB), :] = x_pack[pl.ds(aligned(top + s), SUB), lane(g)].astype(F32)

        def conv_norm(s):
            conv = []
            for g in range(groups):
                acc = xs[q, g, pl.ds(s + 13, SUB), :] * row(0, g) + row(7, g)
                for k in range(1, 7):
                    acc = acc + xs[q, g, pl.ds(s + 13 + k, SUB), :] * row(k, g)
                conv.append(acc)
            mean = jnp.sum(sum(conv), axis=-1, keepdims=True) * inv_c
            cent = [v - mean for v in conv]
            var = jnp.sum(sum([v * v for v in cent]), axis=-1, keepdims=True) * inv_c
            inv = lax.rsqrt(var + eps_norm)
            rs[q, pl.ds(s, SUB), :] = jnp.broadcast_to(inv, (SUB, LANES))
            for g in range(groups):
                nhat = cent[g] * inv
                nh[q, g, pl.ds(s, SUB), :] = nhat
                nrm[pl.ds(s, SUB), lane(g)] = (nhat * row(8, g) + row(9, g)).astype(BF)
                dyf = dy_pack[pl.ds(aligned(top + dy_lead + s), SUB), lane(g)].astype(F32)
                dzs[pl.ds(s, SUB), lane(g)] = (dyf * row(11, g)).astype(BF)

        tasks = []
        lead = 2 * TILE
        for s in range(0, lead, SUB):
            tasks.append(functools.partial(ingest, s))
        for s in range(0, R, SUB):
            tasks.append(functools.partial(ingest, s + lead))
            tasks.append(functools.partial(conv_norm, s))
        return tasks

    def post_tasks(b, q):
        top = b * R

        def norm_back(s):
            dn, prod = [], []
            for g in range(groups):
                bv = br[pl.ds(s, SUB), lane(g)]
                x_mid = xs[q, g, pl.ds(s + TILE, SUB), :]
                ob = (x_mid + row(10, g)) + bv * row(12, g)
                ob_pack[pl.ds(aligned(top + ob_lead + s), SUB), lane(g)] = ob.astype(BF)
                d2 = dn2[pl.ds(s, SUB), lane(g)]
                nhat = nh[q, g, pl.ds(s, SUB), :]
                dg = d2 * row(13, g)
                dn.append(dg)
                prod.append(dg * nhat)
                if grads:
                    p2 = d2 * nhat
                    dyf = dy_pack[pl.ds(aligned(top + dy_lead + s), SUB), lane(g)].astype(F32)
                    dyb = dyf * bv
                    sm_acc[g, 8] += p2[0:8] + p2[8:16]
                    sm_acc[g, 9] += d2[0:8] + d2[8:16]
                    sm_acc[g, 10] += dyf[0:8] + dyf[8:16]
                    sm_acc[g, 11] += dyb[0:8] + dyb[8:16]
            m1 = jnp.sum(sum(dn), axis=-1, keepdims=True) * inv_c
            m2 = jnp.sum(sum(prod), axis=-1, keepdims=True) * inv_c
            inv = rs[q, pl.ds(s, SUB), :]
            for g in range(groups):
                nhat = nh[q, g, pl.ds(s, SUB), :]
                dconv = inv * (dn[g] - m1 - nhat * m2)
                ds[g, pl.ds(2 * TILE + s, SUB), :] = dconv
                if grads:
                    sm_acc[g, 7] += dconv[0:8] + dconv[8:16]
                    for k in range(7):
                        tp = dconv * xs[q, g, pl.ds(s + 13 + k, SUB), :]
                        sm_acc[g, k] += tp[0:8] + tp[8:16]

        def carry():
            for g in range(groups):
                ds[g, pl.ds(0, 2 * TILE), :] = ds[g, pl.ds(R, 2 * TILE), :]

        return [carry] + [functools.partial(norm_back, s) for s in range(0, R, SUB)]

    def frame_tasks(b):
        top = b * R

        def frames_back(s):
            for g in range(groups):
                acc = dy_pack[pl.ds(aligned(top + R + s), SUB), lane(g)].astype(F32)
                for k in range(7):
                    acc = acc + ds[g, pl.ds(s + 19 - k, SUB), :] * row(k, g)
                gb_pack[pl.ds(aligned(top + R + s), SUB), lane(g)] = acc.astype(BF)

        return [functools.partial(frames_back, s) for s in range(0, R, SUB)]

    def up_step(c):
        cols = slice(c * HCHUNK, (c + 1) * HCHUNK)

        def one():
            pre_s[c % 2] = dot_nt(nrm[...], w_e[cols, :])

        def two():
            dh_s[c % 2] = dot_nt(dzs[...], w_p[cols, :])

        return [one, two]

    def gelu_tasks(c):
        cols = slice(c * HCHUNK, (c + 1) * HCHUNK)

        def part(s):
            u = pre_s[c % 2, pl.ds(s, SUB), :] + pb[0:1, cols]
            v = 1.0 + lax.erf(u)
            hid[pl.ds(s, SUB), cols] = (u * v).astype(BF)
            e = jnp.exp2(SLOPE_LOG - LOG2E * (u * u))
            dp2 = dh_s[c % 2, pl.ds(s, SUB), :] * (v + u * e)
            dpre[pl.ds(s, SUB), cols] = dp2.astype(BF)
            if grads:
                gb_acc[:, cols] += dp2[0:8] + dp2[8:16]

        return [functools.partial(part, s) for s in range(0, R, SUB)]

    def down_steps():
        steps = []
        for h in range(2):
            cols = slice(h * (width // 2), (h + 1) * (width // 2))

            def one(cols=cols):
                br[:, cols] = dot_nn(hid[...], w_p[:, cols])

            def two(cols=cols):
                dn2[:, cols] = dot_nn(dpre[...], w_e[:, cols])

            steps += [one, two]
        return steps

    def grad_steps():
        steps = []

        def turn():
            left_t[0] = nrm[...].T
            left_t[1] = dzs[...].T

        for c in range(hidden // HCHUNK):
            cols = slice(c * HCHUNK, (c + 1) * HCHUNK)
            for which, right in enumerate((dpre, hid)):

                def step(which=which, right=right, cols=cols):
                    gacc[which, :, cols] += dot_nn(left_t[which], right[:, cols])

                steps.append(step)
        return turn, steps

    def interleave(steps, tasks):
        done = 0
        for index, step in enumerate(steps):
            step()
            upto = len(tasks) * (index + 1) // len(steps)
            while done < upto:
                tasks[done]()
                done += 1

    def merge(first_list, second_list):
        total = [(index / len(part), which, task) for which, part in enumerate((first_list, second_list)) for index, task in enumerate(part)]
        return [task for _, _, task in sorted(total, key=lambda item: item[:2])]

    def run_tasks(tasks):
        for task in tasks:
            task()

    for k in range(n):

        @pl.when(off[k] < R + TILE)
        def _():
            clip_ready(k)

    run_tasks(conv_tasks(0, 0))
    for copy in w_copies:
        copy.wait()
    n_chunk = hidden // HCHUNK

    @pl.loop(0, nblk)
    def _(i):
        q = lax.rem(i, 2)
        for k in range(n):

            @pl.when((off[k] >= (i + 1) * R + TILE) & (off[k] < (i + 2) * R + TILE))
            def _():
                clip_ready(k)

        post = post_tasks(i - 1, 1 - q)
        for c in range(n_chunk):
            mine = post[len(post) * c // n_chunk : len(post) * (c + 1) // n_chunk]
            interleave(up_step(c), merge(gelu_tasks(c - 1), mine) if c else mine)
        run_tasks(gelu_tasks(n_chunk - 1))
        rest = merge(conv_tasks(i + 1, 1 - q), frame_tasks(i - 1))
        if grads:
            turn, steps = grad_steps()
            turn()
            interleave(down_steps() + steps, rest)
        else:
            interleave(down_steps(), rest)

        if n_recv:

            @pl.when(i == 0)
            def _():
                for copy in recv_in:
                    copy.wait()
                for copy in recv_out:
                    copy.start()

        for k in range(n):
            end = off[k] + len_of[k] + TILE

            @pl.when((end > (i - 1) * R) & (end <= i * R))
            def _():
                clip_done(k)

    run_tasks(post_tasks(nblk - 1, lax.rem(nblk - 1, 2)))
    run_tasks(frame_tasks(nblk - 1))
    for k in range(n):

        @pl.when(off[k] + len_of[k] + TILE > (nblk - 1) * R)
        def _():
            clip_done(k)

    if grads:
        share = hidden // parts
        piece = math.gcd(share, HCHUNK)
        for which in range(2):
            for c in range(hidden // HCHUNK):
                cols = slice(c * HCHUNK, (c + 1) * HCHUNK)
                turned = (gacc[which, :, cols] * ROOT_HALF).T.astype(BF)
                for h in range(0, HCHUNK, piece):
                    t_of, r_of = divmod(c * HCHUNK + h, share)
                    for g in range(groups):
                        g_out[t_of % 2, t_of // 2, g, which, pl.ds(r_of, piece), :] = turned[h : h + piece, lane(g)]
        gbias_out[...] = jnp.sum(gb_acc[...], axis=0, keepdims=True) * 0.5
        for g in range(groups):
            for k in range(12):
                small_out[k : k + 1, lane(g)] = jnp.sum(sm_acc[g, k], axis=0, keepdims=True)
    for k in range(n):
        clip_out(k, lambda c: c.wait())
    for copy in recv_out:
        copy.wait()


def run_block(grads, n, base, meta, x, dy, w, chan, bias, held, received, rec_base, parts):
    clips, length, width = x.shape
    hidden = w.shape[2]
    groups = width // LANES
    first = held is None
    R = BLOCK
    rows = n * (length + TILE) + 3 * R + 8 * TILE
    out_shape = [jax.ShapeDtypeStruct((clips, length, width), BF)] * 2 + [
        jax.ShapeDtypeStruct((n, length, width), BF)
    ] * 2
    any_spec = pl.BlockSpec(memory_space=pl.ANY)
    vmem_spec = pl.BlockSpec(memory_space=pltpu.VMEM)
    out_shape.append(jax.ShapeDtypeStruct((8, LANES), F32))
    out_specs = [any_spec] * 4 + [vmem_spec]
    if grads:
        out_shape += [
            jax.ShapeDtypeStruct((2, parts // 2, groups, 2, hidden // parts, LANES), BF),
            jax.ShapeDtypeStruct((12, width), F32),
            jax.ShapeDtypeStruct((1, hidden), F32),
        ]
        out_specs += [vmem_spec] * 3
    args = [meta, x, dy, w, chan, bias]
    in_specs = [
        pl.BlockSpec(memory_space=pltpu.SMEM),
        any_spec,
        any_spec,
        any_spec,
        vmem_spec,
        vmem_spec,
    ]
    aliases = {}
    if not first:
        aliases = {6: 0, 7: 1}
        args += list(held)
        in_specs += [any_spec] * 2
    args += list(received)
    in_specs += [any_spec] * len(received)
    scratch = [pltpu.VMEM((rows, width), BF)] * 4 + [pltpu.VMEM((hidden, width), BF)] * 2
    scratch += [
        pltpu.VMEM((2, groups, R + 2 * TILE, LANES), F32),
        pltpu.VMEM((2, groups, R, LANES), F32),
        pltpu.VMEM((2, R, LANES), F32),
        pltpu.VMEM((groups, R + 2 * TILE, LANES), F32),
    ]
    scratch += [pltpu.VMEM((R, width), BF)] * 2
    scratch += [pltpu.VMEM((R, width), F32)] * 2
    scratch += [pltpu.VMEM((R, hidden), BF)] * 2
    scratch += [pltpu.VMEM((2, R, HCHUNK), F32)] * 2
    scratch += [
        pltpu.VMEM((16, width), F32),
        pltpu.VMEM((1, hidden), F32),
        pltpu.VMEM((length // 2, width), BF),
        pltpu.SemaphoreType.DMA((n, 2, 8)),
        pltpu.SemaphoreType.DMA((n, 4, 16)),
        pltpu.SemaphoreType.DMA((2, groups)),
    ]
    if received:
        rec_n = received[0].shape[0]
        scratch += [pltpu.VMEM((2, rec_n, length, width), BF), pltpu.SemaphoreType.DMA((2, 2, rec_n))]
    if grads:
        scratch += [
            pltpu.VMEM((2, width, hidden), F32),
            pltpu.VMEM((2, width, R), BF),
            pltpu.VMEM((8, hidden), F32),
            pltpu.VMEM((groups, 12, 8, LANES), F32),
        ]
    per_row = 2 * width * hidden * (6 if grads else 4)
    cost = pl.CostEstimate(
        flops=int(per_row * n * length * 1.5), bytes_accessed=n * length * width * 12, transcendentals=0
    )
    return pl.pallas_call(
        functools.partial(block_kernel, grads, first, n, base, len(received), rec_base, parts, length, width, hidden),
        out_shape=tuple(out_shape),
        in_specs=in_specs,
        out_specs=tuple(out_specs),
        scratch_shapes=scratch,
        input_output_aliases=aliases,
        cost_estimate=cost,
        compiler_params=pltpu.CompilerParams(vmem_limit_bytes=56 * MIB),
        name="block_grads" if grads else "block_plain",
    )(*args)


def place_kernel(base, counts, meta, *refs):
    n_in = 2 + 2 * len(counts)
    ins = refs[2:n_in]
    outs = refs[n_in : n_in + 2]
    stage, sem = refs[n_in + 2 :]
    taken, placed = [], []
    at = 0
    for block, count in enumerate(counts):
        for k in range(count):
            for j in range(2):
                taken.append(pltpu.make_async_copy(ins[2 * block + j].at[k], stage.at[j, at], sem.at[0, j, at]))
                placed.append(
                    pltpu.make_async_copy(stage.at[j, at], outs[j].at[meta[16 + base + at]], sem.at[1, j, at])
                )
            at += 1
    for copy in taken:
        copy.start()
    for one, two in zip(taken, placed):
        one.wait()
        two.start()
    for copy in placed:
        copy.wait()


def place_received(base, counts, meta, held, arrays):
    any_spec = pl.BlockSpec(memory_space=pl.ANY)
    length, width = held[0].shape[1:]
    total = sum(counts)
    return pl.pallas_call(
        functools.partial(place_kernel, base, counts),
        out_shape=tuple(jax.ShapeDtypeStruct(h.shape, h.dtype) for h in held),
        in_specs=[pl.BlockSpec(memory_space=pltpu.SMEM)] + [any_spec] * (2 + len(arrays)),
        out_specs=(any_spec,) * 2,
        scratch_shapes=[pltpu.VMEM((2, total, length, width), BF), pltpu.SemaphoreType.DMA((2, 2, total))],
        input_output_aliases={1: 0, 2: 1},
        compiler_params=pltpu.CompilerParams(vmem_limit_bytes=40 * MIB),
        name="place_received",
    )(meta, *held, *arrays)


def swap(value, axis, size, bit):
    return lax.ppermute(value, axis, [(i, i ^ bit) for i in range(size)])


def after(value, token):
    return lax.optimization_barrier((value, token))[0]


def tree_sum(values):
    while len(values) > 1:
        values = [values[i] + values[i + 1] for i in range(0, len(values), 2)]
    return values[0]


def pick(value, index):
    return lax.dynamic_index_in_dim(value, index, 0, keepdims=False)


def spread(value, axis, size, me, step, token):
    got = [swap(pick(value, me ^ k), axis, size, k * step) for k in range(1, value.shape[0])]
    got = [after(v, token) for v in got]
    return tree_sum([pick(value, me).astype(F32)] + [v.astype(F32) for v in got])


def total_over(value, axis, size, step, count, token):
    got = [after(swap(value, axis, size, k * step), token) for k in range(1, count)]
    return tree_sum([value] + got)


def per_device(
    frames,
    cotangent,
    lengths,
    expand_weight,
    expand_first,
    expand_second,
    project_weight,
    project_first,
    project_second,
    hidden_bias,
    hidden_bias_first,
    hidden_bias_second,
    channel_param,
    channel_first,
    channel_second,
    *,
    dp_n,
    t_n,
):
    micro, clips, length, width = frames.shape
    hidden_part = expand_weight.shape[1]
    hidden = hidden_part * t_n
    width_part = expand_weight.shape[0]
    count = micro * clips
    d = lax.axis_index("dp")
    t = lax.axis_index("tensor")

    lens = lengths.reshape(count)
    ids = jnp.arange(count, dtype=jnp.int32)
    ahead = (lens[None, :] > lens[:, None]) | ((lens[None, :] == lens[:, None]) & (ids[None, :] < ids[:, None]))
    rank = jnp.sum(ahead.astype(jnp.int32), axis=1)
    per_core = count // 2
    table = np.zeros((t_n, per_core), np.int32)
    for tt in range(t_n):
        core, chip = tt % 2, tt // 2
        own = [4 * (j // 2) + (3 * (j % 2) if core == 0 else 1 + (j % 2)) for j in range(per_core)]
        pair = [chip, per_core - 1 - chip]
        table[tt] = [own[j] for j in pair] + [own[j] for j in range(per_core) if j not in pair]
    both = np.concatenate([table, table[np.arange(t_n) ^ 1]], axis=1)
    wanted = lax.dynamic_slice_in_dim(jnp.asarray(both), t, 1, 0).reshape(2 * per_core)
    hit = (rank[None, :] == wanted[:, None]).astype(jnp.int32)
    seq = jnp.sum(hit * ids[None, :], axis=1)
    seq_len = jnp.sum(hit * lens[None, :], axis=1)
    meta = jnp.concatenate([seq[:per_core], seq_len[:per_core], seq[per_core:]])

    w_own = jnp.stack([expand_weight.T.astype(BF), project_weight.astype(BF)])
    w_all, bias_all, chan_all = gather_weights(dp_n, t_n, w_own, hidden_bias.reshape(1, hidden_part), channel_param)
    if width_part != LANES:
        w_all = jnp.transpose(w_all, (1, 2, 0, 3)).reshape(2, hidden, width // LANES, LANES)
        w_all = jnp.transpose(w_all, (2, 0, 1, 3))
    bias = bias_all.reshape(1, hidden)
    chan = jnp.transpose(chan_all, (1, 0, 2)).reshape(12, width)

    x = frames.reshape(count, length, width)
    dy = cotangent.reshape(count, length, width)
    calls = [(True, 2), (False, 4), (False, 2)]
    held = None
    base = 0
    pending = []
    starts = []
    tokens = []
    for index, (grads, n) in enumerate(calls):
        early = index >= 2
        outs = run_block(
            grads, n, base, meta, x, dy, w_all, chan, bias, held,
            pending[index - 2] if early else (), starts[index - 2] if early else 0, t_n,
        )
        held = outs[:2]
        pending.append(tuple(swap(o, "tensor", t_n, 1) for o in outs[2:4]))
        starts.append(base)
        tokens.append(outs[4])
        if grads:
            g_part, small_part, gbias_part = outs[5:]
        base += n
    held = place_received(starts[1], [4, 2], meta, held, pending[1] + pending[2])

    if width_part != LANES:
        g_part = g_part.reshape(g_part.shape[:-1] + (LANES // width_part, width_part))
        g_part = jnp.transpose(g_part, (0, 1, 2, 5, 3, 4, 6))
        g_part = g_part.reshape(2, t_n // 2, dp_n, 2, hidden_part, width_part)
    core, chip = lax.rem(t, 2), lax.div(t, 2)
    g = spread(g_part, "tensor", t_n, core, 1, tokens[1]).astype(BF)
    g = spread(g, "tensor", t_n, chip, 2, tokens[2]).astype(BF)
    g = spread(g, "dp", dp_n, d, 1, tokens[2])
    shard_expand = g[0].T
    shard_project = g[1]

    small = jnp.concatenate([small_part.reshape(12 * width), gbias_part.reshape(hidden)])
    small = total_over(small, "tensor", t_n, 1, 2, tokens[1])
    small = total_over(small, "tensor", t_n, 2, t_n // 2, tokens[2])
    small = total_over(small, "dp", dp_n, 1, dp_n, tokens[2])
    g_small = lax.dynamic_slice_in_dim(small[: 12 * width].reshape(12, width), d * width_part, width_part, 1)
    g_bias = lax.dynamic_slice_in_dim(small[12 * width :], t * hidden_part, hidden_part, 0)
    back_sum = g_small[10]
    shard_channel = jnp.concatenate(
        [
            g_small[0:8],
            g_small[8:10] * 0.5,
            (back_sum * channel_param[11])[None],
            (g_small[11] * ROOT_HALF + back_sum * channel_param[10])[None],
        ],
        axis=0,
    )

    e_new, e_first, e_second = adam_update(expand_weight, expand_first, expand_second, shard_expand, 0.02)
    p_new, p_first, p_second = adam_update(project_weight, project_first, project_second, shard_project, 0.01)
    b_new, b_first, b_second = adam_update(hidden_bias, hidden_bias_first, hidden_bias_second, g_bias, 0.1)
    c_new, c_first, c_second = adam_update(channel_param, channel_first, channel_second, shard_channel, 0.2)
    return (
        held[0].reshape(frames.shape),
        held[1].reshape(frames.shape),
        e_new,
        e_first,
        e_second,
        e_new.astype(BF),
        p_new,
        p_first,
        p_second,
        p_new.astype(BF),
        b_new,
        b_first,
        b_second,
        c_new,
        c_first,
        c_second,
    )


def solution(mesh):
    frame_spec = P(None, "dp", None, None)
    e_spec = P("dp", "tensor")
    p_spec = P("tensor", "dp")
    b_spec = P("tensor")
    c_spec = P(None, "dp")
    in_specs = (
        (frame_spec, frame_spec, P(None, "dp")) + (e_spec,) * 3 + (p_spec,) * 3 + (b_spec,) * 3 + (c_spec,) * 3
    )
    out_specs = (frame_spec, frame_spec) + (e_spec,) * 4 + (p_spec,) * 4 + (b_spec,) * 3 + (c_spec,) * 3
    body = functools.partial(per_device, dp_n=mesh.shape["dp"], t_n=mesh.shape["tensor"])
    return jax.shard_map(body, mesh=mesh, in_specs=in_specs, out_specs=out_specs, check_vma=False)
```
